128 devices in a mesh: fac: 32 (over y, x, core), freq: 4 (over z).
Axes of the slice: x: 4, y: 4, z: 4, core: 2. Of those that a mesh axis runs over, the one named last changes fastest.
Arguments:
- right_side: float32 [16, 36864, 128], P('freq', 'fac'), may hold values from -6 to 6
- factors: bfloat16 [36864, 1024], P('fac'), may hold values from -0.03125 to 0.03125
- pair_weight: float32 [16, 36864], P('freq', 'fac'), may hold values from -2 to 2
- second_order: float32 [16, 36864], P('freq', 'fac'), may hold values from -1 to 1
- forward: float32 [16, 16], replicated, may hold values from -3 to 3
- backward: float32 [16, 16], replicated, may hold values from -3 to 3
Outputs:
- amplitude: float32 [16, 36864, 128], P('freq', 'fac')
- sources: float32 [16, 36864, 128], P('freq', 'fac')
The draws below stay inside these ranges and needn't reach their ends.
All inputs are finite; a program needn't handle non-finite values.
Results may differ from the reference program's by a relative error of at most 0.0015.
Values may be sent and summed in bfloat16 or wider, within the bound.
No kernel may reach another device: no remote copies, remote signals or barrier semaphores. Data moves between devices by JAX's collectives and lax.ppermute only.
A program may use at most 64 MiB of HBM per device.

```python
import jax
import jax.numpy as jnp
from jax import lax

NAUX = 1024
NFREQ = 16
COLS = 128
OUTER = 2
INNER = 2
PAIRS = 36864


def steps_of(key, dims, shards, low, largest):
    loudness, own = 1.0, jax.random.fold_in(key, 6)
    for dim, parts in shards:
        heights = jnp.exp(jax.random.uniform(jax.random.fold_in(own, dim), (parts,), jnp.float32, low / len(shards), largest / len(shards)))
        loudness = loudness * jnp.repeat(heights, dims[dim] // parts).reshape([-1 if axis == dim else 1 for axis in range(len(dims))])
    return loudness


def scatter_about(rng, extent, width, limit, split=(), kind=jnp.bfloat16):
    values = width * jax.random.normal(rng, extent, jnp.float32)
    if split:
        values = values * steps_of(rng, extent, split, -0.22, 0.18)
    return jnp.clip(values, -limit, limit).astype(kind)


def setup_inputs(seed: int = 0) -> dict:
    seeds = jax.random.split(jax.random.key(seed), 7)
    return {
        "right_side": scatter_about(seeds[0], (NFREQ, PAIRS, COLS), 1.0, 6.0, ((0, 4), (1, 32)), jnp.float32),
        "factors": scatter_about(seeds[1], (PAIRS, NAUX), PAIRS ** -0.5, 0.03125, ((0, 32),)),
        "pair_weight": jnp.clip(jax.random.uniform(seeds[2], (NFREQ, PAIRS), jnp.float32, -2.0, 2.0) * steps_of(seeds[2], (NFREQ, PAIRS), ((0, 4), (1, 32)), -0.4, 0.0), -2.0, 2.0),
        "second_order": jnp.clip(jax.random.uniform(seeds[3], (NFREQ, PAIRS), jnp.float32, -1.0, 1.0) * steps_of(seeds[3], (NFREQ, PAIRS), ((0, 4), (1, 32)), -0.4, 0.0), -1.0, 1.0),
        "forward": scatter_about(seeds[4], (NFREQ, NFREQ), (NFREQ // 4) ** -0.5, 3.0, (), jnp.float32),
        "backward": scatter_about(seeds[5], (NFREQ, NFREQ), (NFREQ // 4) ** -0.5, 3.0, (), jnp.float32),
    }


def reference(right_side, factors, pair_weight, second_order, forward, backward):
    sources = right_side
    amplitude = sources
    for outer in range(OUTER):
        amplitude = sources
        for inner in range(INNER):
            fresh = []
            for freq in range(NFREQ):
                rounded = amplitude[freq].astype(jnp.bfloat16)
                projection = jnp.dot(factors.T, rounded, preferred_element_type=jnp.float32)
                projected = projection.astype(jnp.bfloat16)
                spread = jnp.dot(factors, projected, preferred_element_type=jnp.float32)
                fresh.append(sources[freq] + pair_weight[freq][:, None] * spread)
            amplitude = jnp.stack(fresh)
        timed = jnp.einsum("tw,wpc->tpc", forward, amplitude, precision=lax.Precision.HIGHEST)
        product = second_order[:, :, None] * timed
        returned = jnp.einsum("wt,tpc->wpc", backward, product, precision=lax.Precision.HIGHEST)
        sources = right_side + returned
    return amplitude, sources
```

```python
import jax
import jax.numpy as jnp
from jax import lax
from jax.sharding import PartitionSpec as P

OUTER = 2
INNER = 2
F32 = jnp.float32
BF16 = jnp.bfloat16
F16 = jnp.float16
SIDE = 4


def place(y, x, k):
    return ((y % SIDE) * SIDE + x % SIDE) * 2 + k


def along(d, first):
    pairs = []
    for y in range(SIDE):
        for x in range(SIDE):
            for k in range(2):
                on_x = (k == 0) == first
                there = place(y, x + d, k) if on_x else place(y + d, x, k)
                pairs.append((place(y, x, k), there))
    return pairs


CORES = [(i, i ^ 1) for i in range(2 * SIDE * SIDE)]


def ring(d):
    return [(z, (z + d) % SIDE) for z in range(SIDE)]


def to_half(value):
    peak = jnp.max(jnp.abs(value))
    power = jnp.ceil(jnp.log2(jnp.maximum(peak, 1e-37))) - 14.0
    return (value * jnp.exp2(-power)).astype(F16), power


def shards(right_side, factors, pair_weight, second_order, forward, backward):
    nf, rows, cols = right_side.shape
    naux = factors.shape[1]
    half = naux // 2
    chunk = half // SIDE
    quarter = rows // SIDE
    wide = nf * cols
    me = lax.axis_index("fac")
    z = lax.axis_index("freq")
    core = me % 2
    chip = me // 2
    spot = jnp.where(core == 0, chip % SIDE, chip // SIDE)
    factors_keep = lax.dynamic_slice(factors, (0, core * half), (rows, half))
    factors_send = lax.dynamic_slice(factors, (0, (1 - core) * half), (rows, half))

    def project(table, rounded):
        return jnp.einsum(
            "pa,fpc->afc", table, rounded, preferred_element_type=F32
        ).reshape(half, wide)

    def reduce_all(amplitude):
        rounded = amplitude.astype(BF16)
        sent = project(factors_send, rounded)
        got = lax.ppermute(sent, "fac", CORES)
        mine = project(factors_keep, rounded) + got
        own = lax.dynamic_slice(mine, (spot * chunk, 0), (chunk, wide))
        for d in (1, 2, 3):
            piece = lax.dynamic_slice(
                mine, (((spot + d) % SIDE) * chunk, 0), (chunk, wide)
            ).astype(BF16)
            own = own + lax.ppermute(piece, "fac", along(d, True)).astype(F32)
        own = own.astype(BF16)
        total = own.astype(F32)
        for d in (1, 2, 3):
            total = total + lax.ppermute(own, "fac", along(d, False)).astype(F32)
        total = total.astype(BF16)
        gathered = jnp.zeros((half, wide), BF16)
        gathered = lax.dynamic_update_slice(gathered, total, (spot * chunk, 0))
        for d in (1, 2, 3):
            piece = lax.ppermute(total, "fac", along(d, True))
            gathered = lax.dynamic_update_slice(
                gathered, piece, (((spot - d) % SIDE) * chunk, 0)
            )
        other = lax.ppermute(gathered, "fac", CORES)
        return gathered, other

    def spread_of(parts):
        gathered, other = parts
        return (
            jnp.einsum("pa,afc->fpc", factors_keep, gathered.reshape(half, nf, cols),
                       preferred_element_type=F32)
            + jnp.einsum("pa,afc->fpc", factors_send, other.reshape(half, nf, cols),
                         preferred_element_type=F32)
        )

    def transpose(pieces, power):
        out = [pieces(0).astype(F32) * jnp.exp2(power)]
        tag = jnp.full((1, 16, cols), power, F16)
        for d in (1, 2, 3):
            load = jnp.concatenate([pieces(d).reshape(1, nf * quarter, cols), tag], axis=1)
            got = lax.ppermute(load, "freq", ring(d))
            scale = jnp.exp2(got[0, nf * quarter, 0].astype(F32))
            out.append(got[0, : nf * quarter].reshape(nf, quarter, cols).astype(F32) * scale)
        return out

    def by_source(d):
        return (z - d) % SIDE

    def by_target(d):
        return (z + d) % SIDE

    weight = pair_weight[:, :, None]
    kernel = [lax.dynamic_slice(second_order, (0, z * quarter), (nf, quarter))]
    for d in (1, 2, 3):
        piece = lax.dynamic_slice(second_order, (0, by_target(d) * quarter), (nf, quarter))
        kernel.append(lax.ppermute(piece, "freq", ring(d)))
    kernel = jnp.concatenate(kernel, axis=0)
    index_in = jnp.concatenate([by_source(d) * nf + jnp.arange(nf) for d in range(SIDE)])
    index_out = jnp.concatenate([by_target(d) * nf + jnp.arange(nf) for d in range(SIDE)])
    table_in = forward[index_in][:, index_in]
    table_out = backward[index_out][:, index_in]

    sources = right_side
    for outer in range(OUTER):
        amplitude = sources
        for inner in range(INNER):
            amplitude = sources + weight * spread_of(reduce_all(amplitude))
        packed, power = to_half(amplitude)
        moved = transpose(
            lambda d: lax.dynamic_slice(
                packed, (0, by_target(d) * quarter, 0), (nf, quarter, cols)
            ),
            power,
        )
        moved = jnp.concatenate(moved, axis=0)
        timed = jnp.einsum("tw,wpc->tpc", table_in, moved, precision=lax.Precision.HIGHEST)
        product = kernel[:, :, None] * timed
        renewed = jnp.einsum("wt,tpc->wpc", table_out, product, precision=lax.Precision.HIGHEST)
        packed, power = to_half(renewed)
        back = transpose(lambda d: packed[d * nf : (d + 1) * nf], power)
        sources = right_side
        returned = jnp.zeros_like(right_side)
        for d in range(SIDE):
            returned = lax.dynamic_update_slice(
                returned, back[d], (0, by_source(d) * quarter, 0)
            )
        sources = right_side + returned
    return (amplitude, sources)


def solution(mesh):
    return jax.shard_map(
        shards,
        mesh=mesh,
        in_specs=(
            P("freq", "fac", None),
            P("fac", None),
            P("freq", "fac"),
            P("freq", "fac"),
            P(),
            P(),
        ),
        out_specs=(P("freq", "fac", None), P("freq", "fac", None)),
        check_vma=False,
    )
```

```python
import jax
import jax.numpy as jnp
from jax import lax
from jax.experimental import pallas as pl
from jax.experimental.pallas import tpu as pltpu
from jax.sharding import PartitionSpec as P

OUTER = 2
INNER = 2
F32 = jnp.float32
BF16 = jnp.bfloat16
F16 = jnp.float16
SIDE = 4
RUN = 16
INTERPRET = False


def place(y, x, k):
    return ((y % SIDE) * SIDE + x % SIDE) * 2 + k


def along(d, first):
    pairs = []
    for y in range(SIDE):
        for x in range(SIDE):
            for k in range(2):
                on_x = (k == 0) == first
                there = place(y, x + d, k) if on_x else place(y + d, x, k)
                pairs.append((place(y, x, k), there))
    return pairs


CORES = [(i, i ^ 1) for i in range(2 * SIDE * SIDE)]


def ring(d):
    return [(z, (z + d) % SIDE) for z in range(SIDE)]


def scale_of(peak):
    power = jnp.ceil(jnp.log2(jnp.maximum(peak, 1e-30))) - 14.0
    return power, jnp.exp2(-power)


def pack_body(z_ref, amp_ref, own_ref, *sent):
    nf, rows, cols = amp_ref.shape
    quarter = rows // SIDE
    groups = quarter // RUN
    z = z_ref[0]
    peak = jnp.max(jnp.abs(amp_ref[0]), axis=0, keepdims=True)
    for f in range(1, nf):
        peak = jnp.maximum(peak, jnp.max(jnp.abs(amp_ref[f]), axis=0, keepdims=True))
    peak = jnp.broadcast_to(jnp.max(peak, axis=1, keepdims=True), (1, cols))
    power, scale = scale_of(peak)
    scale = jnp.broadcast_to(scale, (RUN, cols))
    for d in range(SIDE):
        base = ((z + d) % SIDE) * quarter

        def step(g, carry, d=d, base=base):
            for f in range(nf):
                tile = amp_ref[f, pl.ds(pl.multiple_of(base + g * RUN, RUN), RUN), :]
                spot = pl.ds(pl.multiple_of((g * nf + f) * RUN, RUN), RUN)
                if d == 0:
                    own_ref[spot, :] = tile
                else:
                    sent[d - 1][spot, :] = tile * scale
            return carry

        lax.fori_loop(0, groups, step, 0)
        if d:
            sent[d - 1][nf * quarter :, :] = jnp.broadcast_to(power, (RUN, cols))


def mix_body(own_ref, got1, got2, got3, kernel_ref, into_ref, out_ref, kept, *sent):
    body, cols = own_ref.shape
    block = body * SIDE // kernel_ref.shape[0]
    size = into_ref.shape[1]
    part = size // SIDE
    got = (got1, got2, got3)
    gains = [jnp.exp2(jnp.broadcast_to(g[body : body + 1, :], (part, cols))) for g in got]

    def apply(table, value):
        high = value.astype(BF16)
        low = (value - high.astype(F32)).astype(BF16)
        both = jnp.dot(table[...], high, preferred_element_type=F32)
        rest = jnp.dot(table[:size, :], low, preferred_element_type=F32)
        return both[:size] + (both[size:] + rest)

    def step(g, peaks):
        sides = []
        kernels = []
        for half in range(2):
            at = pl.ds(pl.multiple_of((2 * g + half) * part, part), part)
            sides.append(
                jnp.concatenate(
                    [own_ref[at, :]] + [r[at, :] * s for r, s in zip(got, gains)], axis=0
                )
            )
            kernels.append(
                kernel_ref[pl.ds(pl.multiple_of((2 * g + half) * size, size), size), :]
            )
        timed = apply(into_ref, jnp.concatenate(sides, axis=1))
        renewed = apply(out_ref, jnp.concatenate(kernels, axis=1) * timed)
        fresh = list(peaks)
        for half in range(2):
            at = pl.ds(pl.multiple_of((2 * g + half) * part, part), part)
            for d in range(SIDE):
                tile = renewed[d * part : (d + 1) * part, half * cols : (half + 1) * cols]
                if d == 0:
                    kept[at, :] = tile
                else:
                    sent[d - 1][at, :] = tile
                    fresh[d - 1] = jnp.maximum(fresh[d - 1], jnp.abs(tile))
        return tuple(fresh)

    start = tuple(jnp.zeros((part, cols), F32) for _ in range(3))
    peaks = lax.fori_loop(0, body // part // 2, step, start)
    for ref, peak in zip(sent, peaks):
        peak = jnp.max(jnp.max(peak, axis=0, keepdims=True), axis=1, keepdims=True)
        power, scale = scale_of(jnp.broadcast_to(peak, (1, cols)))
        ref[:body, :] = ref[:body, :] * jnp.broadcast_to(scale, (body, cols))
        ref[body:, :] = jnp.broadcast_to(power, (RUN, cols))


def unpack_body(z_ref, right_ref, own_ref, got1, got2, got3, sources_ref, rounded_ref):
    nf, rows, cols = right_ref.shape
    quarter = rows // SIDE
    groups = quarter // RUN
    body = nf * quarter
    z = z_ref[0]
    for d, ref in enumerate((own_ref, got1, got2, got3)):
        base = ((z - d + SIDE) % SIDE) * quarter
        if d:
            gain = jnp.exp2(jnp.broadcast_to(ref[body : body + 1, :], (RUN, cols)))

        def step(g, carry, d=d, base=base, ref=ref, gain=gain if d else None):
            for f in range(nf):
                tile = ref[pl.ds(pl.multiple_of((g * nf + f) * RUN, RUN), RUN), :]
                if d:
                    tile = tile * gain
                at = pl.ds(pl.multiple_of(base + g * RUN, RUN), RUN)
                tile = right_ref[f, at, :] + tile
                sources_ref[f, at, :] = tile
                rounded_ref[f, at, :] = tile.astype(BF16)
            return carry

        lax.fori_loop(0, groups, step, 0)


def call(body, outs, name, scalars=0, args=()):
    spec = pl.BlockSpec(memory_space=pltpu.VMEM)
    flat = pl.BlockSpec(memory_space=pltpu.SMEM)
    return pl.pallas_call(
        body,
        out_shape=[jax.ShapeDtypeStruct(s, t) for s, t in outs],
        in_specs=[flat] * scalars + [spec] * (len(args) - scalars),
        out_specs=[spec] * len(outs),
        compiler_params=pltpu.CompilerParams(vmem_limit_bytes=40 << 20),
        interpret=INTERPRET,
        name=name,
    )(*args)


def shards(right_side, factors, pair_weight, second_order, forward, backward):
    nf, rows, cols = right_side.shape
    naux = factors.shape[1]
    half = naux // 2
    chunk = half // SIDE
    quarter = rows // SIDE
    wide = nf * cols
    me = lax.axis_index("fac")
    z = lax.axis_index("freq")
    core = me % 2
    chip = me // 2
    spot = jnp.where(core == 0, chip % SIDE, chip // SIDE)
    factors_keep = lax.dynamic_slice(factors, (0, core * half), (rows, half))
    factors_send = lax.dynamic_slice(factors, (0, (1 - core) * half), (rows, half))

    def project(table, rounded):
        return jnp.einsum(
            "pa,fpc->afc", table, rounded, preferred_element_type=F32
        ).reshape(half, wide)

    def reduce_all(rounded):
        sent = project(factors_send, rounded)
        got = lax.ppermute(sent, "fac", CORES)
        mine = project(factors_keep, rounded) + got
        own = lax.dynamic_slice(mine, (spot * chunk, 0), (chunk, wide))
        for d in (1, 2, 3):
            piece = lax.dynamic_slice(
                mine, (((spot + d) % SIDE) * chunk, 0), (chunk, wide)
            ).astype(BF16)
            own = own + lax.ppermute(piece, "fac", along(d, True)).astype(F32)
        own = own.astype(BF16)
        total = own.astype(F32)
        for d in (1, 2, 3):
            total = total + lax.ppermute(own, "fac", along(d, False)).astype(F32)
        total = total.astype(BF16)
        gathered = jnp.zeros((half, wide), BF16)
        gathered = lax.dynamic_update_slice(gathered, total, (spot * chunk, 0))
        for d in (1, 2, 3):
            piece = lax.ppermute(total, "fac", along(d, True))
            gathered = lax.dynamic_update_slice(
                gathered, piece, (((spot - d) % SIDE) * chunk, 0)
            )
        other = lax.ppermute(gathered, "fac", CORES)
        return gathered, other

    def spread_of(parts):
        gathered, other = parts
        return (
            jnp.einsum("pa,afc->fpc", factors_keep, gathered.reshape(half, nf, cols),
                       preferred_element_type=F32)
            + jnp.einsum("pa,afc->fpc", factors_send, other.reshape(half, nf, cols),
                         preferred_element_type=F32)
        )

    def exchange(sent):
        return [
            lax.ppermute(load.astype(F16), "freq", ring(d + 1)).astype(F32)
            for d, load in enumerate(sent)
        ]

    body = nf * quarter
    size = SIDE * nf * RUN
    weight = pair_weight[:, :, None]
    place_z = jnp.full((1,), z, jnp.int32)
    kernel = [lax.dynamic_slice(second_order, (0, z * quarter), (nf, quarter))]
    for d in (1, 2, 3):
        piece = lax.dynamic_slice(
            second_order, (0, ((z + d) % SIDE) * quarter), (nf, quarter)
        )
        kernel.append(lax.ppermute(piece, "freq", ring(d)))
    kernel = jnp.concatenate(kernel, axis=0).reshape(SIDE * nf, quarter // RUN, RUN)
    kernel = kernel.transpose(1, 0, 2).reshape(body * SIDE, 1)
    kernel = jnp.broadcast_to(kernel, (body * SIDE, cols))

    row = jnp.arange(size)
    ring_at, f_at = row // (nf * RUN), row // RUN % nf
    names = jnp.arange(SIDE * nf)
    source = (((z - ring_at) % SIDE) * nf + f_at)[:, None] == names[None, :]
    target = (((z + ring_at) % SIDE) * nf + f_at)[:, None] == names[None, :]
    same = (row % RUN)[:, None] == (row % RUN)[None, :]

    def spread_table(left, table, right):
        left, right = left.astype(F32), right.astype(F32)
        full = jnp.einsum("it,tw,jw->ij", left, table, right, precision=lax.Precision.HIGHEST)
        full = jnp.where(same, full, 0.0)
        high = lax.reduce_precision(full, 8, 7)
        return jnp.concatenate([high, full - high], axis=0).astype(BF16)

    table_in = spread_table(source, forward, source)
    table_out = spread_table(target, backward, source)
    loads = [((body, cols), F32)] + [((body + RUN, cols), F32)] * 3

    sources = right_side
    rounded = right_side.astype(BF16)
    for outer in range(OUTER):
        for inner in range(INNER):
            amplitude = sources + weight * spread_of(reduce_all(rounded))
            rounded = amplitude.astype(BF16)
        own, *sent = call(pack_body, loads, "pack", 1, (place_z, amplitude))
        got = exchange(sent)
        own, *sent = call(mix_body, loads, "mix", 0, (own, *got, kernel, table_in, table_out))
        got = exchange(sent)
        sources, rounded = call(
            unpack_body,
            [(right_side.shape, F32), (right_side.shape, BF16)],
            "unpack", 1, (place_z, right_side, own, *got),
        )
    return (amplitude, sources)


def solution(mesh):
    return jax.shard_map(
        shards,
        mesh=mesh,
        in_specs=(
            P("freq", "fac", None),
            P("fac", None),
            P("freq", "fac"),
            P("freq", "fac"),
            P(),
            P(),
        ),
        out_specs=(P("freq", "fac", None), P("freq", "fac", None)),
        check_vma=False,
    )
```

```python
import jax
import jax.numpy as jnp
from jax import lax
from jax.experimental import pallas as pl
from jax.experimental.pallas import tpu as pltpu
from jax.sharding import PartitionSpec as P

OUTER = 2
INNER = 2
F32 = jnp.float32
BF16 = jnp.bfloat16
F16 = jnp.float16
SIDE = 4
RUN = 16
INTERPRET = False


def place(y, x, k):
    return (y * SIDE + x) * 2 + k


def along(d, first):
    pairs = []
    for y in range(SIDE):
        for x in range(SIDE):
            for k in range(2):
                on_x = (k == 0) == first
                there = place(y, x ^ d, k) if on_x else place(y ^ d, x, k)
                pairs.append((place(y, x, k), there))
    return pairs


CORES = [(i, i ^ 1) for i in range(2 * SIDE * SIDE)]


def swap(d):
    return [(z, z ^ d) for z in range(SIDE)]


def scale_of(peak):
    power = jnp.ceil(jnp.log2(jnp.maximum(peak, 1e-30))) - 14.0
    return power, jnp.exp2(-power)


def pack_body(z_ref, amp_ref, own_ref, *sent):
    nf, rows, cols = amp_ref.shape
    quarter = rows // SIDE
    groups = quarter // RUN
    z = z_ref[0]
    peak = jnp.max(jnp.abs(amp_ref[0]), axis=0, keepdims=True)
    for f in range(1, nf):
        peak = jnp.maximum(peak, jnp.max(jnp.abs(amp_ref[f]), axis=0, keepdims=True))
    peak = jnp.broadcast_to(jnp.max(peak, axis=1, keepdims=True), (1, cols))
    power, scale = scale_of(peak)
    scale = jnp.broadcast_to(scale, (RUN, cols))
    for d in range(SIDE):
        base = (z ^ d) * quarter

        def step(g, carry, d=d, base=base):
            for f in range(nf):
                tile = amp_ref[f, pl.ds(pl.multiple_of(base + g * RUN, RUN), RUN), :]
                spot = pl.ds(pl.multiple_of((g * nf + f) * RUN, RUN), RUN)
                if d == 0:
                    own_ref[spot, :] = tile
                else:
                    sent[d - 1][spot, :] = tile * scale
            return carry

        lax.fori_loop(0, groups, step, 0)
        if d:
            sent[d - 1][nf * quarter :, :] = jnp.broadcast_to(power, (RUN, cols))


def mix_body(own_ref, got1, got2, got3, kernel_ref, into_ref, out_ref, kept, *sent):
    body, cols = own_ref.shape
    block = body * SIDE // kernel_ref.shape[0]
    size = into_ref.shape[1]
    part = size // SIDE
    got = (got1, got2, got3)
    gains = [jnp.exp2(jnp.broadcast_to(g[body : body + 1, :], (part, cols))) for g in got]

    def apply(table, value):
        high = value.astype(BF16)
        low = (value - high.astype(F32)).astype(BF16)
        both = jnp.dot(table[...], high, preferred_element_type=F32)
        rest = jnp.dot(table[:size, :], low, preferred_element_type=F32)
        return both[:size] + (both[size:] + rest)

    def step(g, peaks):
        sides = []
        kernels = []
        for half in range(2):
            at = pl.ds(pl.multiple_of((2 * g + half) * part, part), part)
            sides.append(
                jnp.concatenate(
                    [own_ref[at, :]] + [r[at, :] * s for r, s in zip(got, gains)], axis=0
                )
            )
            kernels.append(
                kernel_ref[pl.ds(pl.multiple_of((2 * g + half) * size, size), size), :]
            )
        timed = apply(into_ref, jnp.concatenate(sides, axis=1))
        renewed = apply(out_ref, jnp.concatenate(kernels, axis=1) * timed)
        fresh = list(peaks)
        for half in range(2):
            at = pl.ds(pl.multiple_of((2 * g + half) * part, part), part)
            for d in range(SIDE):
                tile = renewed[d * part : (d + 1) * part, half * cols : (half + 1) * cols]
                if d == 0:
                    kept[at, :] = tile
                else:
                    sent[d - 1][at, :] = tile
                    fresh[d - 1] = jnp.maximum(fresh[d - 1], jnp.abs(tile))
        return tuple(fresh)

    start = tuple(jnp.zeros((part, cols), F32) for _ in range(3))
    peaks = lax.fori_loop(0, body // part // 2, step, start)
    for ref, peak in zip(sent, peaks):
        peak = jnp.max(jnp.max(peak, axis=0, keepdims=True), axis=1, keepdims=True)
        power, scale = scale_of(jnp.broadcast_to(peak, (1, cols)))
        ref[:body, :] = ref[:body, :] * jnp.broadcast_to(scale, (body, cols))
        ref[body:, :] = jnp.broadcast_to(power, (RUN, cols))


def unpack_body(z_ref, right_ref, own_ref, got1, got2, got3, sources_ref, rounded_ref):
    nf, rows, cols = right_ref.shape
    quarter = rows // SIDE
    groups = quarter // RUN
    body = nf * quarter
    z = z_ref[0]
    for d, ref in enumerate((own_ref, got1, got2, got3)):
        base = (z ^ d) * quarter
        if d:
            gain = jnp.exp2(jnp.broadcast_to(ref[body : body + 1, :], (RUN, cols)))

        def step(g, carry, d=d, base=base, ref=ref, gain=gain if d else None):
            for f in range(nf):
                tile = ref[pl.ds(pl.multiple_of((g * nf + f) * RUN, RUN), RUN), :]
                if d:
                    tile = tile * gain
                at = pl.ds(pl.multiple_of(base + g * RUN, RUN), RUN)
                tile = right_ref[f, at, :] + tile
                sources_ref[f, at, :] = tile
                rounded_ref[f, at, :] = tile.astype(BF16)
            return carry

        lax.fori_loop(0, groups, step, 0)


def call(body, outs, name, scalars=0, args=()):
    spec = pl.BlockSpec(memory_space=pltpu.VMEM)
    flat = pl.BlockSpec(memory_space=pltpu.SMEM)
    return pl.pallas_call(
        body,
        out_shape=[jax.ShapeDtypeStruct(s, t) for s, t in outs],
        in_specs=[flat] * scalars + [spec] * (len(args) - scalars),
        out_specs=[spec] * len(outs),
        compiler_params=pltpu.CompilerParams(vmem_limit_bytes=40 << 20),
        interpret=INTERPRET,
        name=name,
    )(*args)


def shards(right_side, factors, pair_weight, second_order, forward, backward):
    nf, rows, cols = right_side.shape
    naux = factors.shape[1]
    half = naux // 2
    chunk = half // SIDE
    quarter = rows // SIDE
    wide = nf * cols
    me = lax.axis_index("fac")
    z = lax.axis_index("freq")
    core = me % 2
    chip = me // 2
    spot = jnp.where(core == 0, chip % SIDE, chip // SIDE)
    factors_keep = lax.dynamic_slice(factors, (0, core * half), (rows, half))
    factors_send = lax.dynamic_slice(factors, (0, (1 - core) * half), (rows, half))

    def project(table, rounded):
        return jnp.einsum(
            "pa,fpc->afc", table, rounded, preferred_element_type=F32
        ).reshape(half, wide)

    def reduce_all(rounded):
        sent = project(factors_send, rounded)
        got = lax.ppermute(sent, "fac", CORES)
        mine = project(factors_keep, rounded) + got
        own = lax.dynamic_slice(mine, (spot * chunk, 0), (chunk, wide))
        for d in (1, 2, 3):
            piece = lax.dynamic_slice(
                mine, ((spot ^ d) * chunk, 0), (chunk, wide)
            ).astype(BF16)
            own = own + lax.ppermute(piece, "fac", along(d, True)).astype(F32)
        own = own.astype(BF16)
        total = own.astype(F32)
        for d in (1, 2, 3):
            total = total + lax.ppermute(own, "fac", along(d, False)).astype(F32)
        total = total.astype(BF16)
        gathered = jnp.zeros((half, wide), BF16)
        gathered = lax.dynamic_update_slice(gathered, total, (spot * chunk, 0))
        for d in (1, 2, 3):
            piece = lax.ppermute(total, "fac", along(d, True))
            gathered = lax.dynamic_update_slice(
                gathered, piece, ((spot ^ d) * chunk, 0)
            )
        other = lax.ppermute(gathered, "fac", CORES)
        return gathered, other

    def spread_of(parts):
        gathered, other = parts
        return (
            jnp.einsum("pa,afc->fpc", factors_keep, gathered.reshape(half, nf, cols),
                       preferred_element_type=F32)
            + jnp.einsum("pa,afc->fpc", factors_send, other.reshape(half, nf, cols),
                         preferred_element_type=F32)
        )

    def exchange(sent):
        return [
            lax.ppermute(load.astype(F16), "freq", swap(d + 1)).astype(F32)
            for d, load in enumerate(sent)
        ]

    body = nf * quarter
    size = SIDE * nf * RUN
    weight = pair_weight[:, :, None]
    place_z = jnp.full((1,), z, jnp.int32)
    kernel = [lax.dynamic_slice(second_order, (0, z * quarter), (nf, quarter))]
    for d in (1, 2, 3):
        piece = lax.dynamic_slice(
            second_order, (0, (z ^ d) * quarter), (nf, quarter)
        )
        kernel.append(lax.ppermute(piece, "freq", swap(d)))
    kernel = jnp.concatenate(kernel, axis=0).reshape(SIDE * nf, quarter // RUN, RUN)
    kernel = kernel.transpose(1, 0, 2).reshape(body * SIDE, 1)
    kernel = jnp.broadcast_to(kernel, (body * SIDE, cols))

    row = jnp.arange(size)
    ring_at, f_at = row // (nf * RUN), row // RUN % nf
    names = jnp.arange(SIDE * nf)
    source = ((z ^ ring_at) * nf + f_at)[:, None] == names[None, :]
    same = (row % RUN)[:, None] == (row % RUN)[None, :]

    def spread_table(left, table, right):
        left, right = left.astype(F32), right.astype(F32)
        full = jnp.einsum("it,tw,jw->ij", left, table, right, precision=lax.Precision.HIGHEST)
        full = jnp.where(same, full, 0.0)
        high = lax.reduce_precision(full, 8, 7)
        return jnp.concatenate([high, full - high], axis=0).astype(BF16)

    table_in = spread_table(source, forward, source)
    table_out = spread_table(source, backward, source)
    loads = [((body, cols), F32)] + [((body + RUN, cols), F32)] * 3

    sources = right_side
    rounded = right_side.astype(BF16)
    for outer in range(OUTER):
        for inner in range(INNER):
            amplitude = sources + weight * spread_of(reduce_all(rounded))
            rounded = amplitude.astype(BF16)
        own, *sent = call(pack_body, loads, "pack", 1, (place_z, amplitude))
        got = exchange(sent)
        own, *sent = call(mix_body, loads, "mix", 0, (own, *got, kernel, table_in, table_out))
        got = exchange(sent)
        sources, rounded = call(
            unpack_body,
            [(right_side.shape, F32), (right_side.shape, BF16)],
            "unpack", 1, (place_z, right_side, own, *got),
        )
    return (amplitude, sources)


def solution(mesh):
    return jax.shard_map(
        shards,
        mesh=mesh,
        in_specs=(
            P("freq", "fac", None),
            P("fac", None),
            P("freq", "fac"),
            P("freq", "fac"),
            P(),
            P(),
        ),
        out_specs=(P("freq", "fac", None), P("freq", "fac", None)),
        check_vma=False,
    )
```

```python
from functools import partial

import jax
import jax.numpy as jnp
from jax import lax
from jax.experimental import pallas as pl
from jax.experimental.pallas import tpu as pltpu
from jax.sharding import PartitionSpec as P

OUTER = 2
INNER = 2
F32 = jnp.float32
BF16 = jnp.bfloat16
F16 = jnp.float16
SIDE = 4
RUN = 16
INTERPRET = False


def place(y, x, k):
    return (y * SIDE + x) * 2 + k


def along(d, first):
    pairs = []
    for y in range(SIDE):
        for x in range(SIDE):
            for k in range(2):
                on_x = (k == 0) == first
                there = place(y, x ^ d, k) if on_x else place(y ^ d, x, k)
                pairs.append((place(y, x, k), there))
    return pairs


CORES = [(i, i ^ 1) for i in range(2 * SIDE * SIDE)]


def swap(d):
    return [(z, z ^ d) for z in range(SIDE)]


def scale_of(peak):
    power = jnp.ceil(jnp.log2(jnp.maximum(peak, 1e-30))) - 14.0
    return power, jnp.exp2(-power)


def round_body(right_ref, rounded_ref):
    nf, rows, cols = right_ref.shape
    for f in range(nf):
        rounded_ref[:, f * cols : (f + 1) * cols] = right_ref[f].astype(BF16)


def gather_parts(core_ref, mine_ref, other_ref, whole):
    half = mine_ref.shape[0]
    core = core_ref[0]
    whole[pl.ds(pl.multiple_of(core * half, half), half), :] = mine_ref[...]
    whole[pl.ds(pl.multiple_of((1 - core) * half, half), half), :] = other_ref[...]


def ladder_body(core_ref, factors_ref, mine_ref, other_ref, sources_ref, weight_ref,
                rounded_ref, whole):
    nf, rows, cols = sources_ref.shape
    gather_parts(core_ref, mine_ref, other_ref, whole)
    span = rows // SIDE

    def step(r, carry):
        at = pl.ds(pl.multiple_of(r * span, RUN), span)
        spread = jnp.dot(factors_ref[at, :], whole[...], preferred_element_type=F32)
        for f in range(nf):
            lanes = slice(f * cols, (f + 1) * cols)
            value = sources_ref[f, at, :] + weight_ref[at, f : f + 1] * spread[:, lanes]
            rounded_ref[at, lanes] = value.astype(BF16)
        return carry

    lax.fori_loop(0, SIDE, step, 0)


def pack_body(offset, core_ref, z_ref, factors_ref, mine_ref, other_ref, sources_ref,
              weight_ref, sent_ref, whole):
    nf, rows, cols = sources_ref.shape
    quarter = rows // SIDE
    body = sent_ref.shape[1] - RUN
    length = body // nf
    gather_parts(core_ref, mine_ref, other_ref, whole)

    def block(d, peak):
        base = pl.multiple_of((z_ref[0] ^ d) * quarter + offset, RUN)
        at = pl.ds(base, length)
        spread = jnp.dot(factors_ref[at, :], whole[...], preferred_element_type=F32)
        for f in range(nf):
            value = sources_ref[f, at, :] + weight_ref[at, f : f + 1] * spread[:, f * cols : (f + 1) * cols]
            for g in range(length // RUN):
                tile = value[g * RUN : (g + 1) * RUN]
                sent_ref[d, (g * nf + f) * RUN : (g * nf + f + 1) * RUN, :] = tile
                peak = jnp.maximum(peak, jnp.abs(tile))
        return peak

    peak = lax.fori_loop(0, SIDE, block, jnp.zeros((RUN, cols), F32))
    peak = jnp.max(jnp.max(peak, axis=0, keepdims=True), axis=1, keepdims=True)
    power, scale = scale_of(jnp.broadcast_to(peak, (1, cols)))
    for d in range(1, SIDE):
        sent_ref[d, :body, :] = sent_ref[d, :body, :] * jnp.broadcast_to(scale, (body, cols))
        sent_ref[d, body:, :] = jnp.broadcast_to(power, (RUN, cols))


def mix_body(own_ref, got1, got2, got3, kernel_ref, into_ref, out_ref, sent_ref):
    cols = own_ref.shape[2]
    body = own_ref.shape[1] - RUN
    size = into_ref.shape[1]
    part = size // SIDE
    got = (got1, got2, got3)
    gains = [jnp.exp2(jnp.broadcast_to(g[body : body + 1, :], (part, cols))) for g in got]

    def apply(table, value):
        high = value.astype(BF16)
        low = (value - high.astype(F32)).astype(BF16)
        both = jnp.dot(table[...], high, preferred_element_type=F32)
        rest = jnp.dot(table[:size, :], low, preferred_element_type=F32)
        return both[:size] + (both[size:] + rest)

    def step(g, peaks):
        sides = []
        kernels = []
        for half in range(2):
            at = pl.ds(pl.multiple_of((2 * g + half) * part, part), part)
            sides.append(
                jnp.concatenate(
                    [own_ref[0, at, :]] + [r[at, :] * s for r, s in zip(got, gains)], axis=0
                )
            )
            kernels.append(
                kernel_ref[pl.ds(pl.multiple_of((2 * g + half) * size, size), size), :]
            )
        timed = apply(into_ref, jnp.concatenate(sides, axis=1))
        renewed = apply(out_ref, jnp.concatenate(kernels, axis=1) * timed)
        fresh = list(peaks)
        for half in range(2):
            at = pl.ds(pl.multiple_of((2 * g + half) * part, part), part)
            for d in range(SIDE):
                tile = renewed[d * part : (d + 1) * part, half * cols : (half + 1) * cols]
                sent_ref[d, at, :] = tile
                if d:
                    fresh[d - 1] = jnp.maximum(fresh[d - 1], jnp.abs(tile))
        return tuple(fresh)

    start = tuple(jnp.zeros((part, cols), F32) for _ in range(3))
    peaks = lax.fori_loop(0, body // part // 2, step, start)
    for d, peak in enumerate(peaks, 1):
        peak = jnp.max(jnp.max(peak, axis=0, keepdims=True), axis=1, keepdims=True)
        power, scale = scale_of(jnp.broadcast_to(peak, (1, cols)))
        sent_ref[d, :body, :] = sent_ref[d, :body, :] * jnp.broadcast_to(scale, (body, cols))
        sent_ref[d, body:, :] = jnp.broadcast_to(power, (RUN, cols))


def unpack_body(splits, z_ref, right_ref, *refs):
    nf, rows, cols = right_ref.shape
    quarter = rows // SIDE
    z = z_ref[0]
    sources_ref, rounded_ref = refs[-2:]
    for h, (offset, length) in enumerate(splits):
        body = nf * length
        for d, ref in enumerate(refs[h * SIDE : (h + 1) * SIDE]):
            base = (z ^ d) * quarter + offset
            gain = jnp.exp2(jnp.broadcast_to(ref[body : body + 1, :], (RUN, cols))) if d else None

            def step(g, carry, d=d, base=base, ref=ref, gain=gain):
                at = pl.ds(pl.multiple_of(base + g * RUN, RUN), RUN)
                for f in range(nf):
                    spot = pl.ds(pl.multiple_of((g * nf + f) * RUN, RUN), RUN)
                    tile = ref[spot, :] * gain if d else ref[0, spot, :]
                    tile = right_ref[f, at, :] + tile
                    sources_ref[f, at, :] = tile
                    rounded_ref[at, f * cols : (f + 1) * cols] = tile.astype(BF16)
                return carry

            lax.fori_loop(0, length // RUN, step, 0)


def call(body, outs, name, scalars=0, args=(), scratch=()):
    spec = pl.BlockSpec(memory_space=pltpu.VMEM)
    flat = pl.BlockSpec(memory_space=pltpu.SMEM)
    return pl.pallas_call(
        body,
        out_shape=[jax.ShapeDtypeStruct(s, t) for s, t in outs],
        in_specs=[flat] * scalars + [spec] * (len(args) - scalars),
        out_specs=[spec] * len(outs),
        scratch_shapes=list(scratch),
        compiler_params=pltpu.CompilerParams(vmem_limit_bytes=40 << 20),
        interpret=INTERPRET,
        name=name,
    )(*args)


def shards(right_side, factors, pair_weight, second_order, forward, backward):
    nf, rows, cols = right_side.shape
    naux = factors.shape[1]
    half = naux // 2
    chunk = half // SIDE
    quarter = rows // SIDE
    wide = nf * cols
    me = lax.axis_index("fac")
    z = lax.axis_index("freq")
    core = me % 2
    chip = me // 2
    spot = jnp.where(core == 0, chip % SIDE, chip // SIDE)
    factors_keep = lax.dynamic_slice(factors, (0, core * half), (rows, half))
    factors_send = lax.dynamic_slice(factors, (0, (1 - core) * half), (rows, half))

    def project(table, rounded):
        return lax.dot_general(
            table, rounded, (((0,), (0,)), ((), ())), preferred_element_type=F32
        )

    def reduce_all(rounded):
        sent = project(factors_send, rounded)
        got = lax.ppermute(sent, "fac", CORES)
        mine = project(factors_keep, rounded) + got
        own = lax.dynamic_slice(mine, (spot * chunk, 0), (chunk, wide))
        for d in (1, 2, 3):
            piece = lax.dynamic_slice(
                mine, ((spot ^ d) * chunk, 0), (chunk, wide)
            ).astype(BF16)
            own = own + lax.ppermute(piece, "fac", along(d, True)).astype(F32)
        own = own.astype(BF16)
        total = own.astype(F32)
        for d in (1, 2, 3):
            total = total + lax.ppermute(own, "fac", along(d, False)).astype(F32)
        total = total.astype(BF16)
        gathered = jnp.zeros((half, wide), BF16)
        gathered = lax.dynamic_update_slice(gathered, total, (spot * chunk, 0))
        for d in (1, 2, 3):
            piece = lax.ppermute(total, "fac", along(d, True))
            gathered = lax.dynamic_update_slice(
                gathered, piece, ((spot ^ d) * chunk, 0)
            )
        other = lax.ppermute(gathered, "fac", CORES)
        return gathered, other

    def spread_of(parts):
        gathered, other = parts
        return (
            jnp.einsum("pa,afc->fpc", factors_keep, gathered.reshape(half, nf, cols),
                       preferred_element_type=F32)
            + jnp.einsum("pa,afc->fpc", factors_send, other.reshape(half, nf, cols),
                         preferred_element_type=F32)
        )

    def exchange(sent):
        return [
            lax.ppermute(sent[d].astype(F16), "freq", swap(d)).astype(F32)
            for d in range(1, SIDE)
        ]

    body = nf * quarter
    size = SIDE * nf * RUN
    weight = pair_weight[:, :, None]
    place_z = jnp.full((1,), z, jnp.int32)
    kernel = [lax.dynamic_slice(second_order, (0, z * quarter), (nf, quarter))]
    for d in (1, 2, 3):
        piece = lax.dynamic_slice(
            second_order, (0, (z ^ d) * quarter), (nf, quarter)
        )
        kernel.append(lax.ppermute(piece, "freq", swap(d)))
    kernel = jnp.concatenate(kernel, axis=0).reshape(SIDE * nf, quarter // RUN, RUN)
    kernel = kernel.transpose(1, 0, 2).reshape(body * SIDE, 1)
    kernel = jnp.broadcast_to(kernel, (body * SIDE, cols))

    row = jnp.arange(size)
    ring_at, f_at = row // (nf * RUN), row // RUN % nf
    names = jnp.arange(SIDE * nf)
    source = ((z ^ ring_at) * nf + f_at)[:, None] == names[None, :]
    same = (row % RUN)[:, None] == (row % RUN)[None, :]

    def spread_table(left, table, right):
        left, right = left.astype(F32), right.astype(F32)
        full = jnp.einsum("it,tw,jw->ij", left, table, right, precision=lax.Precision.HIGHEST)
        full = jnp.where(same, full, 0.0)
        high = lax.reduce_precision(full, 8, 7)
        return jnp.concatenate([high, full - high], axis=0).astype(BF16)

    table_in = spread_table(source, forward, source)
    table_out = spread_table(source, backward, source)
    loads = [((body, cols), F32)] + [((body + RUN, cols), F32)] * 3

    core_at = jnp.full((1,), core, jnp.int32)
    column = pair_weight.T
    whole = [pltpu.VMEM((naux, wide), BF16)]
    pair = 2 * RUN
    first = (quarter // pair + 1) // 2 * pair
    splits = ((0, first), (first, quarter - first))

    sources = right_side
    (rounded,) = call(round_body, [((rows, wide), BF16)], "round", 0, (right_side,))
    for outer in range(OUTER):
        for inner in range(INNER - 1):
            parts = reduce_all(rounded)
            (rounded,) = call(
                ladder_body, [((rows, wide), BF16)], "ladder", 1,
                (core_at, factors, *parts, sources, column), whole,
            )
        parts = reduce_all(rounded)
        packed = []
        for offset, length in splits:
            body = nf * length
            loads = [((SIDE, body + RUN, cols), F32)]
            (sent,) = call(
                partial(pack_body, offset), loads, "pack", 2,
                (core_at, place_z, factors, *parts, sources, column), whole,
            )
            packed.append((sent, exchange(sent)))
        back = []
        for (offset, length), (own, got) in zip(splits, packed):
            body = nf * length
            loads = [((SIDE, body + RUN, cols), F32)]
            (sent,) = call(
                mix_body, loads, "mix", 0,
                (own, *got, kernel[offset * nf * SIDE : (offset + length) * nf * SIDE],
                 table_in, table_out),
            )
            back += [sent, *exchange(sent)]
        if outer == OUTER - 1:
            amplitude = sources + weight * spread_of(parts)
        sources, rounded = call(
            partial(unpack_body, splits),
            [(right_side.shape, F32), ((rows, wide), BF16)],
            "unpack", 1, (place_z, right_side, *back),
        )
    return (amplitude, sources)


def solution(mesh):
    return jax.shard_map(
        shards,
        mesh=mesh,
        in_specs=(
            P("freq", "fac", None),
            P("fac", None),
            P("freq", "fac"),
            P("freq", "fac"),
            P(),
            P(),
        ),
        out_specs=(P("freq", "fac", None), P("freq", "fac", None)),
        check_vma=False,
    )
```

```python
import jax
import jax.numpy as jnp
from jax import lax
from jax.experimental import pallas as pl
from jax.experimental.pallas import tpu as pltpu
from jax.sharding import PartitionSpec as P

OUTER = 2
INNER = 2
F32 = jnp.float32
BF16 = jnp.bfloat16
F16 = jnp.float16
SIDE = 4
RUN = 16
LANES = 128
PARTNERS = (2, 1, 3)
INTERPRET = False


def place(y, x, k):
    return (y * SIDE + x) * 2 + k


def along(d, first):
    pairs = []
    for y in range(SIDE):
        for x in range(SIDE):
            for k in range(2):
                on_x = (k == 0) == first
                there = place(y, x ^ d, k) if on_x else place(y ^ d, x, k)
                pairs.append((place(y, x, k), there))
    return pairs


CORES = [(i, i ^ 1) for i in range(2 * SIDE * SIDE)]


def swap(d):
    return [(z, z ^ d) for z in range(SIDE)]


def scale_of(peak):
    power = jnp.ceil(jnp.log2(jnp.maximum(peak, 1e-30))) - 14.0
    return power, jnp.exp2(-power)


def round_body(right_ref, rounded_ref):
    nf, rows, cols = right_ref.shape
    for f in range(nf):
        rounded_ref[:, f * cols : (f + 1) * cols] = right_ref[f].astype(BF16)


def gather_parts(core_ref, mine_ref, other_ref, whole):
    half = mine_ref.shape[0]
    core = core_ref[0]
    whole[pl.ds(pl.multiple_of(core * half, half), half), :] = mine_ref[...]
    whole[pl.ds(pl.multiple_of((1 - core) * half, half), half), :] = other_ref[...]


def ladder_body(core_ref, factors_ref, mine_ref, other_ref, sources_ref, weight_ref,
                rounded_ref, whole):
    nf, rows, cols = sources_ref.shape
    gather_parts(core_ref, mine_ref, other_ref, whole)
    span = rows // SIDE

    def step(r, carry):
        at = pl.ds(pl.multiple_of(r * span, RUN), span)
        spread = jnp.dot(factors_ref[at, :], whole[...], preferred_element_type=F32)
        for f in range(nf):
            lanes = slice(f * cols, (f + 1) * cols)
            value = sources_ref[f, at, :] + weight_ref[at, f : f + 1] * spread[:, lanes]
            rounded_ref[at, lanes] = value.astype(BF16)
        return carry

    lax.fori_loop(0, SIDE, step, 0)


def pack_body(core_ref, z_ref, factors_ref, mine_ref, other_ref, sources_ref,
              weight_ref, kernel_ref, sent_ref, whole):
    nf, rows, cols = sources_ref.shape
    quarter = rows // SIDE
    length = quarter
    body = nf * length
    gather_parts(core_ref, mine_ref, other_ref, whole)

    def block(d, peak):
        base = pl.multiple_of((z_ref[0] ^ d) * quarter, RUN)
        at = pl.ds(base, length)
        spread = jnp.dot(factors_ref[at, :], whole[...], preferred_element_type=F32)
        for f in range(nf):
            value = sources_ref[f, at, :] + weight_ref[at, f : f + 1] * spread[:, f * cols : (f + 1) * cols]
            for g in range(length // RUN):
                tile = value[g * RUN : (g + 1) * RUN]
                sent_ref[d, (g * nf + f) * RUN : (g * nf + f + 1) * RUN, :] = tile
                peak = jnp.maximum(peak, jnp.abs(tile))
        kernel = kernel_ref[z_ref[0] ^ d]
        high = kernel.astype(BF16).astype(F32)
        sent_ref[d, body + RUN : body + 2 * RUN, :] = high
        sent_ref[d, body + 2 * RUN :, :] = kernel - high
        return peak

    peak = lax.fori_loop(0, SIDE, block, jnp.zeros((RUN, cols), F32))
    peak = jnp.max(jnp.max(peak, axis=0, keepdims=True), axis=1, keepdims=True)
    power, scale = scale_of(jnp.broadcast_to(peak, (1, cols)))
    for d in range(1, SIDE):
        sent_ref[d, :body, :] = sent_ref[d, :body, :] * jnp.broadcast_to(scale, (body, cols))
        sent_ref[d, body : body + RUN, :] = jnp.broadcast_to(power, (RUN, cols))


def mix_body(own_ref, got1, got2, got3, into_ref, out_ref, sent_ref, turned, kernel_ref):
    cols = own_ref.shape[2]
    body = own_ref.shape[1] - 3 * RUN
    size = into_ref.shape[1]
    part = size // SIDE
    got = (got1, got2, got3)
    nf = part // RUN
    groups = body // part
    each = LANES // RUN
    for d, ref in enumerate((own_ref.at[0], *got)):
        table = ref[body + RUN : body + 2 * RUN, :] + ref[body + 2 * RUN :, :]
        turned[d] = table.T
    strips = -(-groups // each)
    for strip in range(strips):

        def expand(j, carry, strip=strip):
            for d in range(SIDE):
                rows = turned[d, pl.ds(pl.multiple_of(j * RUN, RUN), RUN), :]
                for f in range(nf):
                    column = rows[:, f * strips + strip : f * strips + strip + 1]
                    spot = (strip * each + j) * size + (d * nf + f) * RUN
                    kernel_ref[pl.ds(pl.multiple_of(spot, RUN), RUN), :] = jnp.broadcast_to(column, (RUN, cols))
            return carry

        lax.fori_loop(0, min(each, groups - strip * each), expand, 0)
    gains = [jnp.exp2(jnp.broadcast_to(g[body : body + 1, :], (part, cols))) for g in got]

    def apply(table, value):
        high = value.astype(BF16)
        low = (value - high.astype(F32)).astype(BF16)
        both = jnp.dot(table[...], high, preferred_element_type=F32)
        rest = jnp.dot(table[:size, :], low, preferred_element_type=F32)
        return both[:size] + (both[size:] + rest)

    def step(g, peaks):
        sides = []
        kernels = []
        for half in range(2):
            at = pl.ds(pl.multiple_of((2 * g + half) * part, part), part)
            sides.append(
                jnp.concatenate(
                    [own_ref[0, at, :]] + [r[at, :] * s for r, s in zip(got, gains)], axis=0
                )
            )
            kernels.append(
                kernel_ref[pl.ds(pl.multiple_of((2 * g + half) * size, size), size), :]
            )
        timed = apply(into_ref, jnp.concatenate(sides, axis=1))
        renewed = apply(out_ref, jnp.concatenate(kernels, axis=1) * timed)
        fresh = list(peaks)
        for half in range(2):
            at = pl.ds(pl.multiple_of((2 * g + half) * part, part), part)
            for d in range(SIDE):
                tile = renewed[d * part : (d + 1) * part, half * cols : (half + 1) * cols]
                sent_ref[d, at, :] = tile
                if d:
                    fresh[d - 1] = jnp.maximum(fresh[d - 1], jnp.abs(tile))
        return tuple(fresh)

    start = tuple(jnp.zeros((part, cols), F32) for _ in range(3))
    peaks = lax.fori_loop(0, body // part // 2, step, start)
    for d, peak in enumerate(peaks, 1):
        peak = jnp.max(jnp.max(peak, axis=0, keepdims=True), axis=1, keepdims=True)
        power, scale = scale_of(jnp.broadcast_to(peak, (1, cols)))
        sent_ref[d, :body, :] = sent_ref[d, :body, :] * jnp.broadcast_to(scale, (body, cols))
        sent_ref[d, body:, :] = jnp.broadcast_to(power, (RUN, cols))


def unpack_body(z_ref, right_ref, *refs):
    nf, rows, cols = right_ref.shape
    quarter = rows // SIDE
    z = z_ref[0]
    sources_ref, rounded_ref = refs[-2:]
    body = nf * quarter
    for d, ref in enumerate(refs[:SIDE]):
        base = (z ^ d) * quarter
        gain = jnp.exp2(jnp.broadcast_to(ref[body : body + 1, :], (RUN, cols))) if d else None

        def step(g, carry, d=d, base=base, ref=ref, gain=gain):
            at = pl.ds(pl.multiple_of(base + g * RUN, RUN), RUN)
            for f in range(nf):
                spot = pl.ds(pl.multiple_of((g * nf + f) * RUN, RUN), RUN)
                tile = ref[spot, :] * gain if d else ref[0, spot, :]
                tile = right_ref[f, at, :] + tile
                sources_ref[f, at, :] = tile
                rounded_ref[at, f * cols : (f + 1) * cols] = tile.astype(BF16)
            return carry

        lax.fori_loop(0, quarter // RUN, step, 0)


def call(body, outs, name, scalars=0, args=(), scratch=()):
    spec = pl.BlockSpec(memory_space=pltpu.VMEM)
    flat = pl.BlockSpec(memory_space=pltpu.SMEM)
    return pl.pallas_call(
        body,
        out_shape=[jax.ShapeDtypeStruct(s, t) for s, t in outs],
        in_specs=[flat] * scalars + [spec] * (len(args) - scalars),
        out_specs=[spec] * len(outs),
        scratch_shapes=list(scratch),
        compiler_params=pltpu.CompilerParams(vmem_limit_bytes=40 << 20),
        interpret=INTERPRET,
        name=name,
    )(*args)


def shards(right_side, factors, pair_weight, second_order, forward, backward):
    nf, rows, cols = right_side.shape
    naux = factors.shape[1]
    half = naux // 2
    chunk = half // SIDE
    quarter = rows // SIDE
    wide = nf * cols
    me = lax.axis_index("fac")
    z = lax.axis_index("freq")
    core = me % 2
    chip = me // 2
    spot = jnp.where(core == 0, chip % SIDE, chip // SIDE)
    factors_keep = lax.dynamic_slice(factors, (0, core * half), (rows, half))
    factors_send = lax.dynamic_slice(factors, (0, (1 - core) * half), (rows, half))

    def project(table, rounded):
        return lax.dot_general(
            table, rounded, (((0,), (0,)), ((), ())), preferred_element_type=F32
        )

    def reduce_all(rounded):
        sent = project(factors_send, rounded)
        got = lax.ppermute(sent, "fac", CORES)
        mine = project(factors_keep, rounded) + got
        own = lax.dynamic_slice(mine, (spot * chunk, 0), (chunk, wide))
        for d in PARTNERS:
            piece = lax.dynamic_slice(
                mine, ((spot ^ d) * chunk, 0), (chunk, wide)
            ).astype(BF16)
            own = own + lax.ppermute(piece, "fac", along(d, True)).astype(F32)
        own = own.astype(BF16)
        total = own.astype(F32)
        for d in PARTNERS:
            total = total + lax.ppermute(own, "fac", along(d, False)).astype(F32)
        total = total.astype(BF16)
        gathered = jnp.zeros((half, wide), BF16)
        gathered = lax.dynamic_update_slice(gathered, total, (spot * chunk, 0))
        for d in PARTNERS:
            piece = lax.ppermute(total, "fac", along(d, True))
            gathered = lax.dynamic_update_slice(
                gathered, piece, ((spot ^ d) * chunk, 0)
            )
        other = lax.ppermute(gathered, "fac", CORES)
        return gathered, other

    def spread_of(parts):
        gathered, other = parts
        return (
            jnp.einsum("pa,afc->fpc", factors_keep, gathered.reshape(half, nf, cols),
                       preferred_element_type=F32)
            + jnp.einsum("pa,afc->fpc", factors_send, other.reshape(half, nf, cols),
                         preferred_element_type=F32)
        )

    def exchange(sent):
        got = {}
        for d in PARTNERS:
            got[d] = lax.ppermute(sent[d].astype(F16), "freq", swap(d)).astype(F32)
        return [got[d] for d in range(1, SIDE)]

    body = nf * quarter
    size = SIDE * nf * RUN
    weight = pair_weight[:, :, None]
    place_z = jnp.full((1,), z, jnp.int32)
    strips = -(-quarter // LANES)
    kernel = second_order.reshape(nf, SIDE, quarter).transpose(1, 0, 2)
    kernel = jnp.pad(kernel, ((0, 0), (0, 0), (0, strips * LANES - quarter)))
    kernel = kernel.reshape(SIDE, nf * strips, LANES)
    kernel = jnp.pad(kernel, ((0, 0), (0, RUN - nf * strips), (0, 0)))

    row = jnp.arange(size)
    ring_at, f_at = row // (nf * RUN), row // RUN % nf
    names = jnp.arange(SIDE * nf)
    source = ((z ^ ring_at) * nf + f_at)[:, None] == names[None, :]
    same = (row % RUN)[:, None] == (row % RUN)[None, :]

    def spread_table(left, table, right):
        left, right = left.astype(F32), right.astype(F32)
        full = jnp.einsum("it,tw,jw->ij", left, table, right, precision=lax.Precision.HIGHEST)
        full = jnp.where(same, full, 0.0)
        high = lax.reduce_precision(full, 8, 7)
        return jnp.concatenate([high, full - high], axis=0).astype(BF16)

    table_in = spread_table(source, forward, source)
    table_out = spread_table(source, backward, source)

    core_at = jnp.full((1,), core, jnp.int32)
    column = pair_weight.T
    whole = [pltpu.VMEM((naux, wide), BF16)]
    sources = right_side
    (rounded,) = call(round_body, [((rows, wide), BF16)], "round", 0, (right_side,))
    for outer in range(OUTER):
        for inner in range(INNER - 1):
            parts = reduce_all(rounded)
            (rounded,) = call(
                ladder_body, [((rows, wide), BF16)], "ladder", 1,
                (core_at, factors, *parts, sources, column), whole,
            )
        parts = reduce_all(rounded)
        (sent,) = call(
            pack_body, [((SIDE, body + 3 * RUN, cols), F32)], "pack", 2,
            (core_at, place_z, factors, *parts, sources, column, kernel), whole,
        )
        got = exchange(sent)
        (sent,) = call(
            mix_body, [((SIDE, body + RUN, cols), F32)], "mix", 0,
            (sent, *got, table_in, table_out),
            [pltpu.VMEM((SIDE, LANES, RUN), F32), pltpu.VMEM((SIDE * body, cols), F32)],
        )
        back = [sent, *exchange(sent)]
        if outer == OUTER - 1:
            amplitude = sources + weight * spread_of(parts)
        sources, rounded = call(
            unpack_body,
            [(right_side.shape, F32), ((rows, wide), BF16)],
            "unpack", 1, (place_z, right_side, *back),
        )
    return (amplitude, sources)


def solution(mesh):
    return jax.shard_map(
        shards,
        mesh=mesh,
        in_specs=(
            P("freq", "fac", None),
            P("fac", None),
            P("freq", "fac"),
            P("freq", "fac"),
            P(),
            P(),
        ),
        out_specs=(P("freq", "fac", None), P("freq", "fac", None)),
        check_vma=False,
    )
```

```python
from functools import partial

import jax
import jax.numpy as jnp
from jax import lax
from jax.experimental import pallas as pl
from jax.experimental.pallas import tpu as pltpu
from jax.sharding import PartitionSpec as P

OUTER = 2
INNER = 2
F32 = jnp.float32
BF16 = jnp.bfloat16
F16 = jnp.float16
SIDE = 4
RUN = 16
LANES = 128
PARTNERS = (2, 1, 3)
INTERPRET = False


def place(y, x, k):
    return (y * SIDE + x) * 2 + k


def along(d, first):
    pairs = []
    for y in range(SIDE):
        for x in range(SIDE):
            for k in range(2):
                on_x = (k == 0) == first
                there = place(y, x ^ d, k) if on_x else place(y ^ d, x, k)
                pairs.append((place(y, x, k), there))
    return pairs


CORES = [(i, i ^ 1) for i in range(2 * SIDE * SIDE)]


def swap(d):
    return [(z, z ^ d) for z in range(SIDE)]


def scale_of(peak):
    power = jnp.ceil(jnp.log2(jnp.maximum(peak, 1e-30))) - 14.0
    return power, jnp.exp2(-power)


def round_body(right_ref, rounded_ref):
    nf, rows, cols = right_ref.shape
    for f in range(nf):
        rounded_ref[:, f * cols : (f + 1) * cols] = right_ref[f].astype(BF16)


def gather_parts(core_ref, mine_ref, other_ref, whole):
    half = mine_ref.shape[0]
    core = core_ref[0]
    whole[pl.ds(pl.multiple_of(core * half, half), half), :] = mine_ref[...]
    whole[pl.ds(pl.multiple_of((1 - core) * half, half), half), :] = other_ref[...]


def ladder_body(core_ref, factors_ref, mine_ref, other_ref, sources_ref, weight_ref,
                rounded_ref, whole):
    nf, rows, cols = sources_ref.shape
    gather_parts(core_ref, mine_ref, other_ref, whole)
    span = rows // SIDE

    def step(r, carry):
        at = pl.ds(pl.multiple_of(r * span, RUN), span)
        spread = jnp.dot(factors_ref[at, :], whole[...], preferred_element_type=F32)
        for f in range(nf):
            lanes = slice(f * cols, (f + 1) * cols)
            value = sources_ref[f, at, :] + weight_ref[at, f : f + 1] * spread[:, lanes]
            rounded_ref[at, lanes] = value.astype(BF16)
        return carry

    lax.fori_loop(0, SIDE, step, 0)


def pack_body(core_ref, z_ref, factors_ref, mine_ref, other_ref, sources_ref,
              weight_ref, kernel_ref, sent_ref, whole):
    nf, rows, cols = sources_ref.shape
    quarter = rows // SIDE
    length = quarter
    body = nf * length
    gather_parts(core_ref, mine_ref, other_ref, whole)

    def block(d, peak):
        base = pl.multiple_of((z_ref[0] ^ d) * quarter, RUN)
        at = pl.ds(base, length)
        spread = jnp.dot(factors_ref[at, :], whole[...], preferred_element_type=F32)
        for f in range(nf):
            value = sources_ref[f, at, :] + weight_ref[at, f : f + 1] * spread[:, f * cols : (f + 1) * cols]
            for g in range(length // RUN):
                tile = value[g * RUN : (g + 1) * RUN]
                sent_ref[d, (g * nf + f) * RUN : (g * nf + f + 1) * RUN, :] = tile
                peak = jnp.maximum(peak, jnp.abs(tile))
        kernel = kernel_ref[z_ref[0] ^ d]
        high = kernel.astype(BF16).astype(F32)
        sent_ref[d, body + RUN : body + 2 * RUN, :] = high
        sent_ref[d, body + 2 * RUN :, :] = kernel - high
        return peak

    peak = lax.fori_loop(0, SIDE, block, jnp.zeros((RUN, cols), F32))
    peak = jnp.max(jnp.max(peak, axis=0, keepdims=True), axis=1, keepdims=True)
    power, scale = scale_of(jnp.broadcast_to(peak, (1, cols)))
    for d in range(1, SIDE):
        sent_ref[d, :body, :] = sent_ref[d, :body, :] * jnp.broadcast_to(scale, (body, cols))
        sent_ref[d, body : body + RUN, :] = jnp.broadcast_to(power, (RUN, cols))


def mix_body(first, own_ref, got1, got2, got3, into_ref, out_ref, *refs):
    if first:
        sent_ref, kernel_ref, turned = refs
    else:
        kernel_ref, sent_ref = refs
    cols = own_ref.shape[2]
    body = own_ref.shape[1] - 3 * RUN
    size = into_ref.shape[1]
    part = size // SIDE
    got = (got1, got2, got3)
    nf = part // RUN
    groups = body // part
    each = LANES // RUN
    strips = -(-groups // each)
    if first:
        for d, ref in enumerate((own_ref.at[0], *got)):
            table = ref[body + RUN : body + 2 * RUN, :] + ref[body + 2 * RUN :, :]
            turned[d] = table.T
        for strip in range(strips):

            def expand(j, carry, strip=strip):
                for d in range(SIDE):
                    rows = turned[d, pl.ds(pl.multiple_of(j * RUN, RUN), RUN), :]
                    for f in range(nf):
                        column = rows[:, f * strips + strip : f * strips + strip + 1]
                        spot = (strip * each + j) * size + (d * nf + f) * RUN
                        kernel_ref[pl.ds(pl.multiple_of(spot, RUN), RUN), :] = jnp.broadcast_to(column, (RUN, cols))
                return carry

            lax.fori_loop(0, min(each, groups - strip * each), expand, 0)
    wide = 6 if groups % 6 == 0 else 2
    gains = [jnp.exp2(jnp.broadcast_to(g[body : body + 1, :], (part, cols))) for g in got]

    def apply(table, value):
        high = value.astype(BF16)
        low = (value - high.astype(F32)).astype(BF16)
        both = jnp.dot(table[...], high, preferred_element_type=F32)
        rest = jnp.dot(table[:size, :], low, preferred_element_type=F32)
        return both[:size] + (both[size:] + rest)

    def step(g, peaks):
        sides = []
        kernels = []
        for half in range(wide):
            at = pl.ds(pl.multiple_of((wide * g + half) * part, part), part)
            sides.append(
                jnp.concatenate(
                    [own_ref[0, at, :]] + [r[at, :] * s for r, s in zip(got, gains)], axis=0
                )
            )
            kernels.append(
                kernel_ref[pl.ds(pl.multiple_of((wide * g + half) * size, size), size), :]
            )
        timed = apply(into_ref, jnp.concatenate(sides, axis=1))
        renewed = apply(out_ref, jnp.concatenate(kernels, axis=1) * timed)
        fresh = list(peaks)
        for half in range(wide):
            at = pl.ds(pl.multiple_of((wide * g + half) * part, part), part)
            for d in range(SIDE):
                tile = renewed[d * part : (d + 1) * part, half * cols : (half + 1) * cols]
                sent_ref[d, at, :] = tile
                if d:
                    fresh[d - 1] = jnp.maximum(fresh[d - 1], jnp.abs(tile))
        return tuple(fresh)

    start = tuple(jnp.zeros((part, cols), F32) for _ in range(3))
    peaks = lax.fori_loop(0, groups // wide, step, start)
    for d, peak in enumerate(peaks, 1):
        peak = jnp.max(jnp.max(peak, axis=0, keepdims=True), axis=1, keepdims=True)
        power, scale = scale_of(jnp.broadcast_to(peak, (1, cols)))
        sent_ref[d, :body, :] = sent_ref[d, :body, :] * jnp.broadcast_to(scale, (body, cols))
        sent_ref[d, body:, :] = jnp.broadcast_to(power, (RUN, cols))


def unpack_body(z_ref, right_ref, *refs):
    nf, rows, cols = right_ref.shape
    quarter = rows // SIDE
    z = z_ref[0]
    sources_ref, rounded_ref = refs[-2:]
    body = nf * quarter
    for d, ref in enumerate(refs[:SIDE]):
        base = (z ^ d) * quarter
        gain = jnp.exp2(jnp.broadcast_to(ref[body : body + 1, :], (RUN, cols))) if d else None

        def step(g, carry, d=d, base=base, ref=ref, gain=gain):
            at = pl.ds(pl.multiple_of(base + g * RUN, RUN), RUN)
            for f in range(nf):
                spot = pl.ds(pl.multiple_of((g * nf + f) * RUN, RUN), RUN)
                tile = ref[spot, :] * gain if d else ref[0, spot, :]
                tile = right_ref[f, at, :] + tile
                sources_ref[f, at, :] = tile
                rounded_ref[at, f * cols : (f + 1) * cols] = tile.astype(BF16)
            return carry

        lax.fori_loop(0, quarter // RUN, step, 0)


def call(body, outs, name, limit, scalars=0, args=(), scratch=()):
    spec = pl.BlockSpec(memory_space=pltpu.VMEM)
    flat = pl.BlockSpec(memory_space=pltpu.SMEM)
    return pl.pallas_call(
        body,
        out_shape=[jax.ShapeDtypeStruct(s, t) for s, t in outs],
        in_specs=[flat] * scalars + [spec] * (len(args) - scalars),
        out_specs=[spec] * len(outs),
        scratch_shapes=list(scratch),
        compiler_params=pltpu.CompilerParams(vmem_limit_bytes=limit << 20),
        interpret=INTERPRET,
        name=name,
    )(*args)


def shards(right_side, factors, pair_weight, second_order, forward, backward):
    nf, rows, cols = right_side.shape
    naux = factors.shape[1]
    half = naux // 2
    chunk = half // SIDE
    quarter = rows // SIDE
    wide = nf * cols
    me = lax.axis_index("fac")
    z = lax.axis_index("freq")
    core = me % 2
    chip = me // 2
    spot = jnp.where(core == 0, chip % SIDE, chip // SIDE)
    factors_keep = lax.dynamic_slice(factors, (0, core * half), (rows, half))
    factors_send = lax.dynamic_slice(factors, (0, (1 - core) * half), (rows, half))

    def project(table, rounded):
        return lax.dot_general(
            table, rounded, (((0,), (0,)), ((), ())), preferred_element_type=F32
        )

    def reduce_all(rounded):
        sent = project(factors_send, rounded)
        got = lax.ppermute(sent, "fac", CORES)
        mine = project(factors_keep, rounded) + got
        own = lax.dynamic_slice(mine, (spot * chunk, 0), (chunk, wide))
        for d in PARTNERS:
            piece = lax.dynamic_slice(
                mine, ((spot ^ d) * chunk, 0), (chunk, wide)
            ).astype(BF16)
            own = own + lax.ppermute(piece, "fac", along(d, True)).astype(F32)
        own = own.astype(BF16)
        total = own.astype(F32)
        for d in PARTNERS:
            total = total + lax.ppermute(own, "fac", along(d, False)).astype(F32)
        total = total.astype(BF16)
        gathered = jnp.zeros((half, wide), BF16)
        gathered = lax.dynamic_update_slice(gathered, total, (spot * chunk, 0))
        for d in PARTNERS:
            piece = lax.ppermute(total, "fac", along(d, True))
            gathered = lax.dynamic_update_slice(
                gathered, piece, ((spot ^ d) * chunk, 0)
            )
        other = lax.ppermute(gathered, "fac", CORES)
        return gathered, other

    def spread_of(parts):
        gathered, other = parts
        return (
            jnp.einsum("pa,afc->fpc", factors_keep, gathered.reshape(half, nf, cols),
                       preferred_element_type=F32)
            + jnp.einsum("pa,afc->fpc", factors_send, other.reshape(half, nf, cols),
                         preferred_element_type=F32)
        )

    def exchange(sent):
        got = {}
        for d in PARTNERS:
            got[d] = lax.ppermute(sent[d].astype(F16), "freq", swap(d)).astype(F32)
        return [got[d] for d in range(1, SIDE)]

    body = nf * quarter
    size = SIDE * nf * RUN
    weight = pair_weight[:, :, None]
    place_z = jnp.full((1,), z, jnp.int32)
    strips = -(-quarter // LANES)
    kernel = second_order.reshape(nf, SIDE, quarter).transpose(1, 0, 2)
    kernel = jnp.pad(kernel, ((0, 0), (0, 0), (0, strips * LANES - quarter)))
    kernel = kernel.reshape(SIDE, nf * strips, LANES)
    kernel = jnp.pad(kernel, ((0, 0), (0, RUN - nf * strips), (0, 0)))

    row = jnp.arange(size)
    ring_at, f_at = row // (nf * RUN), row // RUN % nf
    names = jnp.arange(SIDE * nf)
    source = ((z ^ ring_at) * nf + f_at)[:, None] == names[None, :]
    same = (row % RUN)[:, None] == (row % RUN)[None, :]

    def spread_table(left, table, right):
        left, right = left.astype(F32), right.astype(F32)
        full = jnp.einsum("it,tw,jw->ij", left, table, right, precision=lax.Precision.HIGHEST)
        full = jnp.where(same, full, 0.0)
        high = lax.reduce_precision(full, 8, 7)
        return jnp.concatenate([high, full - high], axis=0).astype(BF16)

    table_in = spread_table(source, forward, source)
    table_out = spread_table(source, backward, source)

    core_at = jnp.full((1,), core, jnp.int32)
    column = pair_weight.T
    whole = [pltpu.VMEM((naux, wide), BF16)]
    sources = right_side
    (rounded,) = call(round_body, [((rows, wide), BF16)], "round", 4, 0, (right_side,))
    for outer in range(OUTER):
        for inner in range(INNER - 1):
            parts = reduce_all(rounded)
            (rounded,) = call(
                ladder_body, [((rows, wide), BF16)], "ladder", 10, 1,
                (core_at, factors, *parts, sources, column), whole,
            )
        parts = reduce_all(rounded)
        (sent,) = call(
            pack_body, [((SIDE, body + 3 * RUN, cols), F32)], "pack", 12, 2,
            (core_at, place_z, factors, *parts, sources, column, kernel), whole,
        )
        got = exchange(sent)
        mixed = [((SIDE, body + RUN, cols), F32)]
        tables = (table_in, table_out)
        if outer == 0:
            sent, spread_kernel = call(
                partial(mix_body, True), mixed + [((SIDE * body, cols), F32)], "mix", 16, 0,
                (sent, *got, *tables), [pltpu.VMEM((SIDE, LANES, RUN), F32)],
            )
        else:
            (sent,) = call(
                partial(mix_body, False), mixed, "mix", 16, 0,
                (sent, *got, *tables, spread_kernel),
            )
        back = [sent, *exchange(sent)]
        if outer == OUTER - 1:
            amplitude = sources + weight * spread_of(parts)
        sources, rounded = call(
            unpack_body,
            [(right_side.shape, F32), ((rows, wide), BF16)],
            "unpack", 4, 1, (place_z, right_side, *back),
        )
    return (amplitude, sources)


def solution(mesh):
    return jax.shard_map(
        shards,
        mesh=mesh,
        in_specs=(
            P("freq", "fac", None),
            P("fac", None),
            P("freq", "fac"),
            P("freq", "fac"),
            P(),
            P(),
        ),
        out_specs=(P("freq", "fac", None), P("freq", "fac", None)),
        check_vma=False,
    )
```

```python
from functools import partial

import jax
import jax.numpy as jnp
from jax import lax
from jax.experimental import pallas as pl
from jax.experimental.pallas import tpu as pltpu
from jax.sharding import PartitionSpec as P

OUTER = 2
INNER = 2
F32 = jnp.float32
BF16 = jnp.bfloat16
F16 = jnp.float16
SIDE = 4
RUN = 16
LANES = 128
PARTNERS = (2, 1, 3)
INTERPRET = False


def place(y, x, k):
    return (y * SIDE + x) * 2 + k


def along(d, first):
    pairs = []
    for y in range(SIDE):
        for x in range(SIDE):
            for k in range(2):
                on_x = (k == 0) == first
                there = place(y, x ^ d, k) if on_x else place(y ^ d, x, k)
                pairs.append((place(y, x, k), there))
    return pairs


CORES = [(i, i ^ 1) for i in range(2 * SIDE * SIDE)]


def swap(d):
    return [(z, z ^ d) for z in range(SIDE)]


def scale_of(peak):
    power = jnp.ceil(jnp.log2(jnp.maximum(peak, 1e-30))) - 14.0
    return power, jnp.exp2(-power)


def round_body(core_ref, right_ref, keep_ref, send_ref, moved_ref):
    nf, rows, cols = right_ref.shape
    share = nf // 2
    for j in range(share):
        lanes = slice(j * cols, (j + 1) * cols)
        keep_ref[:, lanes] = right_ref[core_ref[0] * share + j].astype(BF16)
        value = right_ref[(1 - core_ref[0]) * share + j]
        send_ref[:, lanes] = value.astype(BF16)
        moved_ref[j] = value


def ladder_body(core_ref, spot_ref, mine_ref, theirs_ref, piece0, piece1, piece2, piece3,
                sources_ref, moved_ref, weight_ref, weight_moved_ref, own_ref, other_ref, whole):
    share, rows, cols = moved_ref.shape
    chunk = piece0.shape[0]
    for d, piece in enumerate((piece0, piece1, piece2, piece3)):
        whole[pl.ds(pl.multiple_of((spot_ref[0] ^ d) * chunk, chunk), chunk), :] = piece[...]
    span = rows // SIDE

    def step(r, carry):
        at = pl.ds(pl.multiple_of(r * span, RUN), span)
        spread = jnp.dot(mine_ref[at, :], whole[...], preferred_element_type=F32)
        for j in range(share):
            lanes = slice(j * cols, (j + 1) * cols)
            base = sources_ref[core_ref[0] * share + j, at, :]
            value = base + weight_ref[at, j : j + 1] * spread[:, lanes]
            own_ref[at, lanes] = value.astype(BF16)
        spread = jnp.dot(theirs_ref[at, :], whole[...], preferred_element_type=F32)
        for j in range(share):
            lanes = slice(j * cols, (j + 1) * cols)
            value = moved_ref[j, at, :] + weight_moved_ref[at, j : j + 1] * spread[:, lanes]
            other_ref[at, lanes] = value.astype(BF16)
        return carry

    lax.fori_loop(0, SIDE, step, 0)


def pack_body(last, core_ref, z_ref, factors_ref, mine_ref, other_ref, sources_ref,
              weight_ref, kernel_ref, sent_ref, *refs):
    if last:
        amplitude_ref, whole = refs
    else:
        (whole,) = refs
    nf, rows, cols = sources_ref.shape
    quarter = rows // SIDE
    body = nf * quarter
    half = mine_ref.shape[1]
    core = core_ref[0]
    whole[:, pl.ds(pl.multiple_of(core * half, half), half)] = mine_ref[...]
    whole[:, pl.ds(pl.multiple_of((1 - core) * half, half), half)] = other_ref[...]

    def block(d, peak):
        base = pl.multiple_of((z_ref[0] ^ d) * quarter, RUN)
        at = pl.ds(base, quarter)
        spread = jnp.dot(factors_ref[at, :], whole[...], preferred_element_type=F32)
        for f in range(nf):
            lanes = slice(f * cols, (f + 1) * cols)
            value = sources_ref[f, at, :] + weight_ref[at, f : f + 1] * spread[:, lanes]
            if last:
                amplitude_ref[f, at, :] = value
            for g in range(quarter // RUN):
                tile = value[g * RUN : (g + 1) * RUN]
                sent_ref[d, (g * nf + f) * RUN : (g * nf + f + 1) * RUN, :] = tile
                peak = jnp.maximum(peak, jnp.abs(tile))
        kernel = kernel_ref[z_ref[0] ^ d]
        high = kernel.astype(BF16).astype(F32)
        sent_ref[d, body + RUN : body + 2 * RUN, :] = high
        sent_ref[d, body + 2 * RUN :, :] = kernel - high
        return peak

    peak = lax.fori_loop(0, SIDE, block, jnp.zeros((RUN, cols), F32))
    peak = jnp.max(jnp.max(peak, axis=0, keepdims=True), axis=1, keepdims=True)
    power, scale = scale_of(jnp.broadcast_to(peak, (1, cols)))
    for d in range(1, SIDE):
        sent_ref[d, :body, :] = sent_ref[d, :body, :] * jnp.broadcast_to(scale, (body, cols))
        sent_ref[d, body : body + RUN, :] = jnp.broadcast_to(power, (RUN, cols))


def mix_body(first, own_ref, got1, got2, got3, into_ref, out_ref, *refs):
    if first:
        sent_ref, kernel_ref, turned = refs
    else:
        kernel_ref, sent_ref = refs
    cols = own_ref.shape[2]
    body = own_ref.shape[1] - 3 * RUN
    size = into_ref.shape[1]
    part = size // SIDE
    got = (got1, got2, got3)
    nf = part // RUN
    groups = body // part
    each = LANES // RUN
    strips = -(-groups // each)
    if first:
        for d, ref in enumerate((own_ref.at[0], *got)):
            table = ref[body + RUN : body + 2 * RUN, :] + ref[body + 2 * RUN :, :]
            turned[d] = table.T
        for strip in range(strips):

            def expand(j, carry, strip=strip):
                for d in range(SIDE):
                    rows = turned[d, pl.ds(pl.multiple_of(j * RUN, RUN), RUN), :]
                    for f in range(nf):
                        column = rows[:, f * strips + strip : f * strips + strip + 1]
                        spot = (strip * each + j) * size + (d * nf + f) * RUN
                        kernel_ref[pl.ds(pl.multiple_of(spot, RUN), RUN), :] = jnp.broadcast_to(column, (RUN, cols))
                return carry

            lax.fori_loop(0, min(each, groups - strip * each), expand, 0)
    wide = 6 if groups % 6 == 0 else 2
    gains = [jnp.exp2(jnp.broadcast_to(g[body : body + 1, :], (part, cols))) for g in got]

    def apply(table, value):
        high = value.astype(BF16)
        low = (value - high.astype(F32)).astype(BF16)
        both = jnp.dot(table[...], high, preferred_element_type=F32)
        rest = jnp.dot(table[:size, :], low, preferred_element_type=F32)
        return both[:size] + (both[size:] + rest)

    def step(g, peaks):
        sides = []
        kernels = []
        for half in range(wide):
            at = pl.ds(pl.multiple_of((wide * g + half) * part, part), part)
            sides.append(
                jnp.concatenate(
                    [own_ref[0, at, :]] + [r[at, :] * s for r, s in zip(got, gains)], axis=0
                )
            )
            kernels.append(
                kernel_ref[pl.ds(pl.multiple_of((wide * g + half) * size, size), size), :]
            )
        timed = apply(into_ref, jnp.concatenate(sides, axis=1))
        renewed = apply(out_ref, jnp.concatenate(kernels, axis=1) * timed)
        fresh = list(peaks)
        for half in range(wide):
            at = pl.ds(pl.multiple_of((wide * g + half) * part, part), part)
            for d in range(SIDE):
                tile = renewed[d * part : (d + 1) * part, half * cols : (half + 1) * cols]
                sent_ref[d, at, :] = tile
                if d:
                    fresh[d - 1] = jnp.maximum(fresh[d - 1], jnp.abs(tile))
        return tuple(fresh)

    start = tuple(jnp.zeros((part, cols), F32) for _ in range(3))
    peaks = lax.fori_loop(0, groups // wide, step, start)
    for d, peak in enumerate(peaks, 1):
        peak = jnp.max(jnp.max(peak, axis=0, keepdims=True), axis=1, keepdims=True)
        power, scale = scale_of(jnp.broadcast_to(peak, (1, cols)))
        sent_ref[d, :body, :] = sent_ref[d, :body, :] * jnp.broadcast_to(scale, (body, cols))
        sent_ref[d, body:, :] = jnp.broadcast_to(power, (RUN, cols))


def unpack_body(last, core_ref, z_ref, right_ref, own_ref, got1, got2, got3, sources_ref, *refs):
    nf, rows, cols = right_ref.shape
    share = nf // 2
    quarter = rows // SIDE
    body = nf * quarter
    for d, ref in enumerate((own_ref, got1, got2, got3)):
        base = (z_ref[0] ^ d) * quarter
        gain = jnp.exp2(jnp.broadcast_to(ref[body : body + 1, :], (RUN, cols))) if d else None

        def step(g, carry, d=d, base=base, ref=ref, gain=gain):
            at = pl.ds(pl.multiple_of(base + g * RUN, RUN), RUN)
            for i in range(nf):
                kept = i < share
                side = core_ref[0] if kept else 1 - core_ref[0]
                f = side * share + i % share
                spot = pl.ds(pl.multiple_of((g * nf + f) * RUN, RUN), RUN)
                tile = ref[spot, :] * gain if d else ref[0, spot, :]
                tile = right_ref[f, at, :] + tile
                sources_ref[f, at, :] = tile
                if not last:
                    keep_ref, send_ref, moved_ref = refs
                    lanes = slice(i % share * cols, (i % share + 1) * cols)
                    (keep_ref if kept else send_ref)[at, lanes] = tile.astype(BF16)
                    if not kept:
                        moved_ref[i % share, at, :] = tile
            return carry

        lax.fori_loop(0, quarter // RUN, step, 0)


def call(body, outs, name, limit, scalars=0, args=(), scratch=()):
    spec = pl.BlockSpec(memory_space=pltpu.VMEM)
    flat = pl.BlockSpec(memory_space=pltpu.SMEM)
    return pl.pallas_call(
        body,
        out_shape=[jax.ShapeDtypeStruct(s, t) for s, t in outs],
        in_specs=[flat] * scalars + [spec] * (len(args) - scalars),
        out_specs=[spec] * len(outs),
        scratch_shapes=list(scratch),
        compiler_params=pltpu.CompilerParams(vmem_limit_bytes=limit << 20),
        interpret=INTERPRET,
        name=name,
    )(*args)


def shards(right_side, factors, pair_weight, second_order, forward, backward):
    nf, rows, cols = right_side.shape
    naux = factors.shape[1]
    share = nf // 2
    half = share * cols
    chunk = naux // SIDE
    quarter = rows // SIDE
    me = lax.axis_index("fac")
    z = lax.axis_index("freq")
    core = me % 2
    chip = me // 2
    spot = jnp.where(core == 0, chip % SIDE, chip // SIDE)

    def project(table, rounded):
        return lax.dot_general(
            table, rounded, (((0,), (0,)), ((), ())), preferred_element_type=F32
        )

    def swap_cores(value):
        return lax.ppermute(value, "fac", CORES)

    def reduce_chips(partial_sum):
        own = lax.dynamic_slice(partial_sum, (spot * chunk, 0), (chunk, half))
        for d in PARTNERS:
            piece = lax.dynamic_slice(
                partial_sum, ((spot ^ d) * chunk, 0), (chunk, half)
            ).astype(BF16)
            own = own + lax.ppermute(piece, "fac", along(d, True)).astype(F32)
        own = own.astype(BF16)
        total = own.astype(F32)
        for d in PARTNERS:
            total = total + lax.ppermute(own, "fac", along(d, False)).astype(F32)
        total = total.astype(BF16)
        pieces = {0: total}
        for d in PARTNERS:
            pieces[d] = lax.ppermute(total, "fac", along(d, True))
        return [pieces[d] for d in range(SIDE)]

    def exchange(sent):
        got = {}
        for d in PARTNERS:
            got[d] = lax.ppermute(sent[d].astype(F16), "freq", swap(d)).astype(F32)
        return [got[d] for d in range(1, SIDE)]

    body = nf * quarter
    size = SIDE * nf * RUN
    place_z = jnp.full((1,), z, jnp.int32)
    strips = -(-quarter // LANES)
    kernel = second_order.reshape(nf, SIDE, quarter).transpose(1, 0, 2)
    kernel = jnp.pad(kernel, ((0, 0), (0, 0), (0, strips * LANES - quarter)))
    kernel = kernel.reshape(SIDE, nf * strips, LANES)
    kernel = jnp.pad(kernel, ((0, 0), (0, RUN - nf * strips), (0, 0)))

    row = jnp.arange(size)
    ring_at, f_at = row // (nf * RUN), row // RUN % nf
    names = jnp.arange(SIDE * nf)
    source = ((z ^ ring_at) * nf + f_at)[:, None] == names[None, :]
    same = (row % RUN)[:, None] == (row % RUN)[None, :]

    def spread_table(left, table, right):
        left, right = left.astype(F32), right.astype(F32)
        full = jnp.einsum("it,tw,jw->ij", left, table, right, precision=lax.Precision.HIGHEST)
        full = jnp.where(same, full, 0.0)
        high = lax.reduce_precision(full, 8, 7)
        return jnp.concatenate([high, full - high], axis=0).astype(BF16)

    table_in = spread_table(source, forward, source)
    table_out = spread_table(source, backward, source)

    core_at = jnp.full((1,), core, jnp.int32)
    spot_at = jnp.full((1,), spot, jnp.int32)
    column = pair_weight.T
    column_mine = lax.dynamic_slice(pair_weight, (core * share, 0), (share, rows)).T
    column_sent = lax.dynamic_slice(pair_weight, ((1 - core) * share, 0), (share, rows))

    sources = right_side
    handed = [((rows, half), BF16), ((rows, half), BF16), ((share, rows, cols), F32)]
    keep, send, moved = call(round_body, handed, "round", 4, 1, (core_at, right_side))
    for outer in range(OUTER):
        last = outer == OUTER - 1
        got = swap_cores(project(factors, send))
        partial_sum = project(factors, keep) + got
        if outer == 0:
            theirs = swap_cores(factors)
            column_moved = swap_cores(column_sent).T
        moved = swap_cores(moved)
        pieces = reduce_chips(partial_sum)
        for inner in range(INNER - 1):
            own, other = call(
                ladder_body, [((rows, half), BF16)] * 2, "ladder", 8, 2,
                (core_at, spot_at, factors, theirs, *pieces, sources, moved,
                 column_mine, column_moved),
                [pltpu.VMEM((naux, half), BF16)],
            )
            pieces = reduce_chips(project(factors, own) + project(theirs, other))
        mine = jnp.zeros((naux, half), BF16)
        for d, piece in enumerate(pieces):
            mine = lax.dynamic_update_slice(mine, piece, ((spot ^ d) * chunk, 0))
        shape = [((SIDE, body + 3 * RUN, cols), F32)]
        if last:
            shape.append((right_side.shape, F32))
        sent, *amplitude = call(
            partial(pack_body, last), shape, "pack", 12, 2,
            (core_at, place_z, factors, mine, swap_cores(mine), sources, column, kernel),
            [pltpu.VMEM((naux, nf * cols), BF16)],
        )
        got = exchange(sent)
        mixed = [((SIDE, body + RUN, cols), F32)]
        tables = (table_in, table_out)
        if outer == 0:
            sent, spread_kernel = call(
                partial(mix_body, True), mixed + [((SIDE * body, cols), F32)], "mix", 16, 0,
                (sent, *got, *tables), [pltpu.VMEM((SIDE, LANES, RUN), F32)],
            )
        else:
            (sent,) = call(
                partial(mix_body, False), mixed, "mix", 16, 0,
                (sent, *got, *tables, spread_kernel),
            )
        sources, *rest = call(
            partial(unpack_body, last), [(right_side.shape, F32)] + ([] if last else handed),
            "unpack", 4, 2, (core_at, place_z, right_side, sent, *exchange(sent)),
        )
        if not last:
            keep, send, moved = rest
    return (amplitude[0], sources)


def solution(mesh):
    return jax.shard_map(
        shards,
        mesh=mesh,
        in_specs=(
            P("freq", "fac", None),
            P("fac", None),
            P("freq", "fac"),
            P("freq", "fac"),
            P(),
            P(),
        ),
        out_specs=(P("freq", "fac", None), P("freq", "fac", None)),
        check_vma=False,
    )
```

```python
from functools import partial

import jax
import jax.numpy as jnp
from jax import lax
from jax.experimental import pallas as pl
from jax.experimental.pallas import tpu as pltpu
from jax.sharding import PartitionSpec as P

OUTER = 2
INNER = 2
F32 = jnp.float32
BF16 = jnp.bfloat16
F16 = jnp.float16
SIDE = 4
RUN = 16
LANES = 128
PARTNERS = (2, 1, 3)
INTERPRET = False


def place(y, x, k):
    return (y * SIDE + x) * 2 + k


def along(d, first):
    pairs = []
    for y in range(SIDE):
        for x in range(SIDE):
            for k in range(2):
                on_x = (k == 0) == first
                there = place(y, x ^ d, k) if on_x else place(y ^ d, x, k)
                pairs.append((place(y, x, k), there))
    return pairs


CORES = [(i, i ^ 1) for i in range(2 * SIDE * SIDE)]


def swap(d):
    return [(z, z ^ d) for z in range(SIDE)]


def scale_of(peak):
    power = jnp.ceil(jnp.log2(jnp.maximum(peak, 1e-30))) - 14.0
    return power, jnp.exp2(-power)


def round_body(right_ref, rounded_ref):
    nf, rows, cols = right_ref.shape
    for f in range(nf):
        rounded_ref[:, f * cols : (f + 1) * cols] = right_ref[f].astype(BF16)


def gather_parts(core_ref, mine_ref, other_ref, whole):
    half = mine_ref.shape[0]
    core = core_ref[0]
    whole[pl.ds(pl.multiple_of(core * half, half), half), :] = mine_ref[...]
    whole[pl.ds(pl.multiple_of((1 - core) * half, half), half), :] = other_ref[...]


def ladder_body(core_ref, factors_ref, mine_ref, other_ref, sources_ref, weight_ref,
                rounded_ref, whole):
    nf, rows, cols = sources_ref.shape
    gather_parts(core_ref, mine_ref, other_ref, whole)
    span = rows // SIDE

    def step(r, carry):
        at = pl.ds(pl.multiple_of(r * span, RUN), span)
        spread = jnp.dot(factors_ref[at, :], whole[...], preferred_element_type=F32)
        for f in range(nf):
            lanes = slice(f * cols, (f + 1) * cols)
            value = sources_ref[f, at, :] + weight_ref[at, f : f + 1] * spread[:, lanes]
            rounded_ref[at, lanes] = value.astype(BF16)
        return carry

    lax.fori_loop(0, SIDE, step, 0)


def pack_body(d, core_ref, z_ref, factors_ref, mine_ref, other_ref, sources_ref,
              weight_ref, kernel_ref, sent_ref, whole):
    nf, rows, cols = sources_ref.shape
    quarter = rows // SIDE
    body = nf * quarter
    gather_parts(core_ref, mine_ref, other_ref, whole)
    there = z_ref[0] ^ d
    at = pl.ds(pl.multiple_of(there * quarter, RUN), quarter)
    spread = jnp.dot(factors_ref[at, :], whole[...], preferred_element_type=F32)
    peak = jnp.zeros((RUN, cols), F32)
    for f in range(nf):
        lanes = slice(f * cols, (f + 1) * cols)
        value = sources_ref[f, at, :] + weight_ref[at, f : f + 1] * spread[:, lanes]
        for g in range(quarter // RUN):
            tile = value[g * RUN : (g + 1) * RUN]
            sent_ref[(g * nf + f) * RUN : (g * nf + f + 1) * RUN, :] = tile
            peak = jnp.maximum(peak, jnp.abs(tile))
    kernel = kernel_ref[there]
    high = kernel.astype(BF16).astype(F32)
    sent_ref[body + RUN : body + 2 * RUN, :] = high
    sent_ref[body + 2 * RUN :, :] = kernel - high
    if d:
        peak = jnp.max(jnp.max(peak, axis=0, keepdims=True), axis=1, keepdims=True)
        power, scale = scale_of(jnp.broadcast_to(peak, (1, cols)))
        sent_ref[:body, :] = sent_ref[:body, :] * jnp.broadcast_to(scale, (body, cols))
        sent_ref[body : body + RUN, :] = jnp.broadcast_to(power, (RUN, cols))


def amplitude_body(core_ref, factors_ref, mine_ref, other_ref, sources_ref, weight_ref,
                   amplitude_ref, whole):
    nf, rows, cols = sources_ref.shape
    gather_parts(core_ref, mine_ref, other_ref, whole)
    span = rows // SIDE

    def step(r, carry):
        at = pl.ds(pl.multiple_of(r * span, RUN), span)
        spread = jnp.dot(factors_ref[at, :], whole[...], preferred_element_type=F32)
        for f in range(nf):
            lanes = slice(f * cols, (f + 1) * cols)
            amplitude_ref[f, at, :] = sources_ref[f, at, :] + weight_ref[at, f : f + 1] * spread[:, lanes]
        return carry

    lax.fori_loop(0, SIDE, step, 0)


def mix_body(first, own_ref, got1, got2, got3, into_ref, out_ref, *refs):
    if first:
        sent_ref, kernel_ref, turned = refs
    else:
        kernel_ref, sent_ref = refs
    body, cols = own_ref.shape[0] - 3 * RUN, own_ref.shape[1]
    size = into_ref.shape[1]
    part = size // SIDE
    got = (got1, got2, got3)
    nf = part // RUN
    groups = body // part
    each = LANES // RUN
    strips = -(-groups // each)
    if first:
        for d, ref in enumerate((own_ref, *got)):
            table = ref[body + RUN : body + 2 * RUN, :] + ref[body + 2 * RUN :, :]
            turned[d] = table.T
        for strip in range(strips):

            def expand(j, carry, strip=strip):
                for d in range(SIDE):
                    rows = turned[d, pl.ds(pl.multiple_of(j * RUN, RUN), RUN), :]
                    for f in range(nf):
                        column = rows[:, f * strips + strip : f * strips + strip + 1]
                        spot = (strip * each + j) * size + (d * nf + f) * RUN
                        kernel_ref[pl.ds(pl.multiple_of(spot, RUN), RUN), :] = jnp.broadcast_to(column, (RUN, cols))
                return carry

            lax.fori_loop(0, min(each, groups - strip * each), expand, 0)
    wide = 6 if groups % 6 == 0 else 2
    gains = [jnp.exp2(jnp.broadcast_to(g[body : body + 1, :], (part, cols))) for g in got]

    def apply(table, value):
        high = value.astype(BF16)
        low = (value - high.astype(F32)).astype(BF16)
        both = jnp.dot(table[...], high, preferred_element_type=F32)
        rest = jnp.dot(table[:size, :], low, preferred_element_type=F32)
        return both[:size] + (both[size:] + rest)

    def step(g, peaks):
        sides = []
        kernels = []
        for half in range(wide):
            at = pl.ds(pl.multiple_of((wide * g + half) * part, part), part)
            sides.append(
                jnp.concatenate(
                    [own_ref[at, :]] + [r[at, :] * s for r, s in zip(got, gains)], axis=0
                )
            )
            kernels.append(
                kernel_ref[pl.ds(pl.multiple_of((wide * g + half) * size, size), size), :]
            )
        timed = apply(into_ref, jnp.concatenate(sides, axis=1))
        renewed = apply(out_ref, jnp.concatenate(kernels, axis=1) * timed)
        fresh = list(peaks)
        for half in range(wide):
            at = pl.ds(pl.multiple_of((wide * g + half) * part, part), part)
            for d in range(SIDE):
                tile = renewed[d * part : (d + 1) * part, half * cols : (half + 1) * cols]
                sent_ref[d, at, :] = tile
                if d:
                    fresh[d - 1] = jnp.maximum(fresh[d - 1], jnp.abs(tile))
        return tuple(fresh)

    start = tuple(jnp.zeros((part, cols), F32) for _ in range(3))
    peaks = lax.fori_loop(0, groups // wide, step, start)
    for d, peak in enumerate(peaks, 1):
        peak = jnp.max(jnp.max(peak, axis=0, keepdims=True), axis=1, keepdims=True)
        power, scale = scale_of(jnp.broadcast_to(peak, (1, cols)))
        sent_ref[d, :body, :] = sent_ref[d, :body, :] * jnp.broadcast_to(scale, (body, cols))
        sent_ref[d, body:, :] = jnp.broadcast_to(power, (RUN, cols))


def unpack_body(z_ref, right_ref, own_ref, got1, got2, got3, sources_ref, *rounded):
    nf, rows, cols = right_ref.shape
    quarter = rows // SIDE
    z = z_ref[0]
    body = nf * quarter
    for d, ref in enumerate((own_ref, got1, got2, got3)):
        base = (z ^ d) * quarter
        gain = jnp.exp2(jnp.broadcast_to(ref[body : body + 1, :], (RUN, cols))) if d else None

        def step(g, carry, d=d, base=base, ref=ref, gain=gain):
            at = pl.ds(pl.multiple_of(base + g * RUN, RUN), RUN)
            for f in range(nf):
                spot = pl.ds(pl.multiple_of((g * nf + f) * RUN, RUN), RUN)
                tile = ref[spot, :] * gain if d else ref[0, spot, :]
                tile = right_ref[f, at, :] + tile
                sources_ref[f, at, :] = tile
                for rounded_ref in rounded:
                    rounded_ref[at, f * cols : (f + 1) * cols] = tile.astype(BF16)
            return carry

        lax.fori_loop(0, quarter // RUN, step, 0)


def call(body, outs, name, limit, scalars=0, args=(), scratch=()):
    spec = pl.BlockSpec(memory_space=pltpu.VMEM)
    flat = pl.BlockSpec(memory_space=pltpu.SMEM)
    return pl.pallas_call(
        body,
        out_shape=[jax.ShapeDtypeStruct(s, t) for s, t in outs],
        in_specs=[flat] * scalars + [spec] * (len(args) - scalars),
        out_specs=[spec] * len(outs),
        scratch_shapes=list(scratch),
        compiler_params=pltpu.CompilerParams(vmem_limit_bytes=limit << 20),
        interpret=INTERPRET,
        name=name,
    )(*args)


def shards(right_side, factors, pair_weight, second_order, forward, backward):
    nf, rows, cols = right_side.shape
    naux = factors.shape[1]
    half = naux // 2
    chunk = half // SIDE
    quarter = rows // SIDE
    wide = nf * cols
    me = lax.axis_index("fac")
    z = lax.axis_index("freq")
    core = me % 2
    chip = me // 2
    spot = jnp.where(core == 0, chip % SIDE, chip // SIDE)
    factors_keep = lax.dynamic_slice(factors, (0, core * half), (rows, half))
    factors_send = lax.dynamic_slice(factors, (0, (1 - core) * half), (rows, half))

    def project(table, rounded):
        return lax.dot_general(
            table, rounded, (((0,), (0,)), ((), ())), preferred_element_type=F32
        )

    def reduce_all(rounded):
        sent = project(factors_send, rounded)
        got = lax.ppermute(sent, "fac", CORES)
        mine = project(factors_keep, rounded) + got
        own = lax.dynamic_slice(mine, (spot * chunk, 0), (chunk, wide))
        for d in PARTNERS:
            piece = lax.dynamic_slice(
                mine, ((spot ^ d) * chunk, 0), (chunk, wide)
            ).astype(BF16)
            own = own + lax.ppermute(piece, "fac", along(d, True)).astype(F32)
        own = own.astype(BF16)
        total = own.astype(F32)
        for d in PARTNERS:
            total = total + lax.ppermute(own, "fac", along(d, False)).astype(F32)
        total = total.astype(BF16)
        gathered = jnp.zeros((half, wide), BF16)
        gathered = lax.dynamic_update_slice(gathered, total, (spot * chunk, 0))
        for d in PARTNERS:
            piece = lax.ppermute(total, "fac", along(d, True))
            gathered = lax.dynamic_update_slice(
                gathered, piece, ((spot ^ d) * chunk, 0)
            )
        other = lax.ppermute(gathered, "fac", CORES)
        return gathered, other

    def exchange(sent):
        got = {}
        for d in PARTNERS:
            got[d] = lax.ppermute(sent[d].astype(F16), "freq", swap(d)).astype(F32)
        return [got[d] for d in range(1, SIDE)]

    body = nf * quarter
    size = SIDE * nf * RUN
    place_z = jnp.full((1,), z, jnp.int32)
    strips = -(-quarter // LANES)
    kernel = second_order.reshape(nf, SIDE, quarter).transpose(1, 0, 2)
    kernel = jnp.pad(kernel, ((0, 0), (0, 0), (0, strips * LANES - quarter)))
    kernel = kernel.reshape(SIDE, nf * strips, LANES)
    kernel = jnp.pad(kernel, ((0, 0), (0, RUN - nf * strips), (0, 0)))

    row = jnp.arange(size)
    ring_at, f_at = row // (nf * RUN), row // RUN % nf
    names = jnp.arange(SIDE * nf)
    source = ((z ^ ring_at) * nf + f_at)[:, None] == names[None, :]
    same = (row % RUN)[:, None] == (row % RUN)[None, :]

    def spread_table(left, table, right):
        left, right = left.astype(F32), right.astype(F32)
        full = jnp.einsum("it,tw,jw->ij", left, table, right, precision=lax.Precision.HIGHEST)
        full = jnp.where(same, full, 0.0)
        high = lax.reduce_precision(full, 8, 7)
        return jnp.concatenate([high, full - high], axis=0).astype(BF16)

    table_in = spread_table(source, forward, source)
    table_out = spread_table(source, backward, source)

    core_at = jnp.full((1,), core, jnp.int32)
    column = pair_weight.T
    whole = [pltpu.VMEM((naux, wide), BF16)]
    sources = right_side
    (rounded,) = call(round_body, [((rows, wide), BF16)], "round", 4, 0, (right_side,))
    for outer in range(OUTER):
        for inner in range(INNER - 1):
            parts = reduce_all(rounded)
            (rounded,) = call(
                ladder_body, [((rows, wide), BF16)], "ladder", 10, 1,
                (core_at, factors, *parts, sources, column), whole,
            )
        parts = reduce_all(rounded)
        sent = {}
        for d in (*PARTNERS, 0):
            (value,) = call(
                partial(pack_body, d), [((body + 3 * RUN, cols), F32)], "pack", 10, 2,
                (core_at, place_z, factors, *parts, sources, column, kernel), whole,
            )
            sent[d] = value
        got = exchange(sent)
        sent = sent[0]
        mixed = [((SIDE, body + RUN, cols), F32)]
        tables = (table_in, table_out)
        if outer == 0:
            sent, spread_kernel = call(
                partial(mix_body, True), mixed + [((SIDE * body, cols), F32)], "mix", 16, 0,
                (sent, *got, *tables), [pltpu.VMEM((SIDE, LANES, RUN), F32)],
            )
        else:
            (sent,) = call(
                partial(mix_body, False), mixed, "mix", 16, 0,
                (sent, *got, *tables, spread_kernel),
            )
        back = [sent, *exchange(sent)]
        last = outer == OUTER - 1
        if last:
            (amplitude,) = call(
                amplitude_body, [(right_side.shape, F32)], "amplitude", 10, 1,
                (core_at, factors, *parts, sources, column), whole,
            )
        sources, *rest = call(
            unpack_body,
            [(right_side.shape, F32)] + ([] if last else [((rows, wide), BF16)]),
            "unpack", 4, 1, (place_z, right_side, *back),
        )
        if not last:
            (rounded,) = rest
    return (amplitude, sources)


def solution(mesh):
    return jax.shard_map(
        shards,
        mesh=mesh,
        in_specs=(
            P("freq", "fac", None),
            P("fac", None),
            P("freq", "fac"),
            P("freq", "fac"),
            P(),
            P(),
        ),
        out_specs=(P("freq", "fac", None), P("freq", "fac", None)),
        check_vma=False,
    )
```

```python
from functools import partial

import jax
import jax.numpy as jnp
from jax import lax
from jax.experimental import pallas as pl
from jax.experimental.pallas import tpu as pltpu
from jax.sharding import PartitionSpec as P

OUTER = 2
INNER = 2
F32 = jnp.float32
BF16 = jnp.bfloat16
F16 = jnp.float16
SIDE = 4
RUN = 16
LANES = 128
PARTNERS = (2, 1, 3)
ARRIVALS = (0, 1, 3, 2)
INTERPRET = False


def place(y, x, k):
    return (y * SIDE + x) * 2 + k


def along(d, first):
    pairs = []
    for y in range(SIDE):
        for x in range(SIDE):
            for k in range(2):
                on_x = (k == 0) == first
                there = place(y, x ^ d, k) if on_x else place(y ^ d, x, k)
                pairs.append((place(y, x, k), there))
    return pairs


CORES = [(i, i ^ 1) for i in range(2 * SIDE * SIDE)]


def swap(d):
    return [(z, z ^ d) for z in range(SIDE)]


def scale_of(peak):
    power = jnp.ceil(jnp.log2(jnp.maximum(peak, 1e-30))) - 14.0
    return power, jnp.exp2(-power)


def round_body(right_ref, rounded_ref):
    nf, rows, cols = right_ref.shape
    for f in range(nf):
        rounded_ref[:, f * cols : (f + 1) * cols] = right_ref[f].astype(BF16)


def gather_parts(core_ref, mine_ref, other_ref, whole):
    half = mine_ref.shape[0]
    core = core_ref[0]
    whole[pl.ds(pl.multiple_of(core * half, half), half), :] = mine_ref[...]
    whole[pl.ds(pl.multiple_of((1 - core) * half, half), half), :] = other_ref[...]


def join_body(spot_ref, piece0, piece1, piece3, piece2, out_ref):
    chunk = piece0.shape[0]
    for d, piece in enumerate((piece0, piece1, piece2, piece3)):
        at = pl.ds(pl.multiple_of((spot_ref[0] ^ d) * chunk, chunk), chunk)
        out_ref[at, :] = piece[...]


def ladder_body(core_ref, factors_ref, mine_ref, other_ref, sources_ref, weight_ref,
                rounded_ref, whole):
    nf, rows, cols = sources_ref.shape
    gather_parts(core_ref, mine_ref, other_ref, whole)
    span = rows // SIDE

    def step(r, carry):
        at = pl.ds(pl.multiple_of(r * span, RUN), span)
        spread = jnp.dot(factors_ref[at, :], whole[...], preferred_element_type=F32)
        for f in range(nf):
            lanes = slice(f * cols, (f + 1) * cols)
            value = sources_ref[f, at, :] + weight_ref[at, f : f + 1] * spread[:, lanes]
            rounded_ref[at, lanes] = value.astype(BF16)
        return carry

    lax.fori_loop(0, SIDE, step, 0)


def pack_body(d, core_ref, z_ref, factors_ref, mine_ref, other_ref, sources_ref,
              weight_ref, kernel_ref, sent_ref, whole):
    nf, rows, cols = sources_ref.shape
    quarter = rows // SIDE
    body = nf * quarter
    there = z_ref[0] ^ d
    at = pl.ds(pl.multiple_of(there * quarter, RUN), quarter)
    gather_parts(core_ref, mine_ref, other_ref, whole)
    spread = jnp.dot(factors_ref[at, :], whole[...], preferred_element_type=F32)
    peak = jnp.zeros((RUN, cols), F32)
    for f in range(nf):
        lanes = slice(f * cols, (f + 1) * cols)
        value = sources_ref[f, at, :] + weight_ref[at, f : f + 1] * spread[:, lanes]
        for g in range(quarter // RUN):
            tile = value[g * RUN : (g + 1) * RUN]
            sent_ref[(g * nf + f) * RUN : (g * nf + f + 1) * RUN, :] = tile
            peak = jnp.maximum(peak, jnp.abs(tile))
    kernel = kernel_ref[there]
    high = kernel.astype(BF16).astype(F32)
    sent_ref[body + RUN : body + 2 * RUN, :] = high
    sent_ref[body + 2 * RUN :, :] = kernel - high
    if d:
        peak = jnp.max(jnp.max(peak, axis=0, keepdims=True), axis=1, keepdims=True)
        power, scale = scale_of(jnp.broadcast_to(peak, (1, cols)))
        sent_ref[:body, :] = sent_ref[:body, :] * jnp.broadcast_to(scale, (body, cols))
        sent_ref[body : body + RUN, :] = jnp.broadcast_to(power, (RUN, cols))


def amplitude_body(core_ref, factors_ref, mine_ref, other_ref, sources_ref, weight_ref,
                   amplitude_ref, whole):
    nf, rows, cols = sources_ref.shape
    gather_parts(core_ref, mine_ref, other_ref, whole)
    span = rows // SIDE

    def step(r, carry):
        at = pl.ds(pl.multiple_of(r * span, RUN), span)
        spread = jnp.dot(factors_ref[at, :], whole[...], preferred_element_type=F32)
        for f in range(nf):
            lanes = slice(f * cols, (f + 1) * cols)
            amplitude_ref[f, at, :] = sources_ref[f, at, :] + weight_ref[at, f : f + 1] * spread[:, lanes]
        return carry

    lax.fori_loop(0, SIDE, step, 0)


def mix_body(first, own_ref, got1, got3, got2, into_ref, out_ref, *refs):
    if first:
        sent_ref, kernel_ref, turned = refs
    else:
        kernel_ref, sent_ref = refs
    body, cols = own_ref.shape[0] - 3 * RUN, own_ref.shape[1]
    size = into_ref.shape[1]
    part = size // SIDE
    got = (got1, got2, got3)
    nf = part // RUN
    groups = body // part
    each = LANES // RUN
    strips = -(-groups // each)
    if first:
        for d, ref in enumerate((own_ref, *got)):
            table = ref[body + RUN : body + 2 * RUN, :] + ref[body + 2 * RUN :, :]
            turned[d] = table.T
        for strip in range(strips):

            def expand(j, carry, strip=strip):
                for d in range(SIDE):
                    rows = turned[d, pl.ds(pl.multiple_of(j * RUN, RUN), RUN), :]
                    for f in range(nf):
                        column = rows[:, f * strips + strip : f * strips + strip + 1]
                        spot = (strip * each + j) * size + (d * nf + f) * RUN
                        kernel_ref[pl.ds(pl.multiple_of(spot, RUN), RUN), :] = jnp.broadcast_to(column, (RUN, cols))
                return carry

            lax.fori_loop(0, min(each, groups - strip * each), expand, 0)
    wide = 6 if groups % 6 == 0 else 2
    gains = [jnp.exp2(jnp.broadcast_to(g[body : body + 1, :], (part, cols))) for g in got]

    def apply(table, value):
        high = value.astype(BF16)
        low = (value - high.astype(F32)).astype(BF16)
        both = jnp.dot(table[...], high, preferred_element_type=F32)
        rest = jnp.dot(table[:size, :], low, preferred_element_type=F32)
        return both[:size] + (both[size:] + rest)

    def step(g, peaks):
        sides = []
        kernels = []
        for half in range(wide):
            at = pl.ds(pl.multiple_of((wide * g + half) * part, part), part)
            sides.append(
                jnp.concatenate(
                    [own_ref[at, :]] + [r[at, :] * s for r, s in zip(got, gains)], axis=0
                )
            )
            kernels.append(
                kernel_ref[pl.ds(pl.multiple_of((wide * g + half) * size, size), size), :]
            )
        timed = apply(into_ref, jnp.concatenate(sides, axis=1))
        renewed = apply(out_ref, jnp.concatenate(kernels, axis=1) * timed)
        fresh = list(peaks)
        for half in range(wide):
            at = pl.ds(pl.multiple_of((wide * g + half) * part, part), part)
            for d in range(SIDE):
                tile = renewed[d * part : (d + 1) * part, half * cols : (half + 1) * cols]
                sent_ref[d, at, :] = tile
                if d:
                    fresh[d - 1] = jnp.maximum(fresh[d - 1], jnp.abs(tile))
        return tuple(fresh)

    start = tuple(jnp.zeros((part, cols), F32) for _ in range(3))
    peaks = lax.fori_loop(0, groups // wide, step, start)
    for d, peak in enumerate(peaks, 1):
        peak = jnp.max(jnp.max(peak, axis=0, keepdims=True), axis=1, keepdims=True)
        power, scale = scale_of(jnp.broadcast_to(peak, (1, cols)))
        sent_ref[d, :body, :] = sent_ref[d, :body, :] * jnp.broadcast_to(scale, (body, cols))
        sent_ref[d, body:, :] = jnp.broadcast_to(power, (RUN, cols))


def unpack_body(z_ref, right_ref, own_ref, got1, got3, got2, sources_ref, *rounded):
    nf, rows, cols = right_ref.shape
    quarter = rows // SIDE
    z = z_ref[0]
    body = nf * quarter
    for d, ref in enumerate((own_ref, got1, got2, got3)):
        base = (z ^ d) * quarter
        gain = jnp.exp2(jnp.broadcast_to(ref[body : body + 1, :], (RUN, cols))) if d else None

        def step(g, carry, d=d, base=base, ref=ref, gain=gain):
            at = pl.ds(pl.multiple_of(base + g * RUN, RUN), RUN)
            for f in range(nf):
                spot = pl.ds(pl.multiple_of((g * nf + f) * RUN, RUN), RUN)
                tile = ref[spot, :] * gain if d else ref[0, spot, :]
                tile = right_ref[f, at, :] + tile
                sources_ref[f, at, :] = tile
                for rounded_ref in rounded:
                    rounded_ref[at, f * cols : (f + 1) * cols] = tile.astype(BF16)
            return carry

        lax.fori_loop(0, quarter // RUN, step, 0)


def call(body, outs, name, limit, scalars=0, args=(), scratch=()):
    spec = pl.BlockSpec(memory_space=pltpu.VMEM)
    flat = pl.BlockSpec(memory_space=pltpu.SMEM)
    specs = [flat] * scalars + [spec] * (len(args) - scalars)
    return pl.pallas_call(
        body,
        out_shape=[jax.ShapeDtypeStruct(s, t) for s, t in outs],
        in_specs=specs,
        out_specs=[spec] * len(outs),
        scratch_shapes=list(scratch),
        compiler_params=pltpu.CompilerParams(vmem_limit_bytes=limit << 20),
        interpret=INTERPRET,
        name=name,
    )(*args)


def shards(right_side, factors, pair_weight, second_order, forward, backward):
    nf, rows, cols = right_side.shape
    naux = factors.shape[1]
    half = naux // 2
    chunk = half // SIDE
    quarter = rows // SIDE
    wide = nf * cols
    me = lax.axis_index("fac")
    z = lax.axis_index("freq")
    core = me % 2
    chip = me // 2
    spot = jnp.where(core == 0, chip % SIDE, chip // SIDE)
    spot_at = jnp.full((1,), spot, jnp.int32)
    factors_keep = lax.dynamic_slice(factors, (0, core * half), (rows, half))
    factors_send = lax.dynamic_slice(factors, (0, (1 - core) * half), (rows, half))

    def project(table, rounded):
        return lax.dot_general(
            table, rounded, (((0,), (0,)), ((), ())), preferred_element_type=F32
        )

    def reduce_all(rounded):
        sent = project(factors_send, rounded)
        got = lax.ppermute(sent, "fac", CORES)
        mine = project(factors_keep, rounded) + got
        own = lax.dynamic_slice(mine, (spot * chunk, 0), (chunk, wide))
        for d in PARTNERS:
            piece = lax.dynamic_slice(
                mine, ((spot ^ d) * chunk, 0), (chunk, wide)
            ).astype(BF16)
            own = own + lax.ppermute(piece, "fac", along(d, True)).astype(F32)
        own = own.astype(BF16)
        total = own.astype(F32)
        for d in PARTNERS:
            total = total + lax.ppermute(own, "fac", along(d, False)).astype(F32)
        total = total.astype(BF16)
        pieces = {0: total}
        for d in PARTNERS:
            pieces[d] = lax.ppermute(total, "fac", along(d, True))
        (gathered,) = call(
            join_body, [((half, wide), BF16)], "join", 4, 1,
            (spot_at, *[pieces[d] for d in ARRIVALS]),
        )
        other = lax.ppermute(gathered, "fac", CORES)
        return gathered, other

    def exchange(sent):
        got = {}
        for d in PARTNERS:
            got[d] = lax.ppermute(sent[d].astype(F16), "freq", swap(d)).astype(F32)
        return [got[d] for d in ARRIVALS[1:]]

    body = nf * quarter
    size = SIDE * nf * RUN
    place_z = jnp.full((1,), z, jnp.int32)
    strips = -(-quarter // LANES)
    kernel = second_order.reshape(nf, SIDE, quarter).transpose(1, 0, 2)
    kernel = jnp.pad(kernel, ((0, 0), (0, 0), (0, strips * LANES - quarter)))
    kernel = kernel.reshape(SIDE, nf * strips, LANES)
    kernel = jnp.pad(kernel, ((0, 0), (0, RUN - nf * strips), (0, 0)))

    row = jnp.arange(size)
    ring_at, f_at = row // (nf * RUN), row // RUN % nf
    names = jnp.arange(SIDE * nf)
    source = ((z ^ ring_at) * nf + f_at)[:, None] == names[None, :]
    same = (row % RUN)[:, None] == (row % RUN)[None, :]

    def spread_table(left, table, right):
        left, right = left.astype(F32), right.astype(F32)
        full = jnp.einsum("it,tw,jw->ij", left, table, right, precision=lax.Precision.HIGHEST)
        full = jnp.where(same, full, 0.0)
        high = lax.reduce_precision(full, 8, 7)
        return jnp.concatenate([high, full - high], axis=0).astype(BF16)

    table_in = spread_table(source, forward, source)
    table_out = spread_table(source, backward, source)

    core_at = jnp.full((1,), core, jnp.int32)
    column = pair_weight.T
    whole = [pltpu.VMEM((naux, wide), BF16)]
    sources = right_side
    (rounded,) = call(round_body, [((rows, wide), BF16)], "round", 4, 0, (right_side,))
    for outer in range(OUTER):
        for inner in range(INNER - 1):
            parts = reduce_all(rounded)
            (rounded,) = call(
                ladder_body, [((rows, wide), BF16)], "ladder", 10, 1,
                (core_at, factors, *parts, sources, column),
                whole,
            )
        parts = reduce_all(rounded)
        sent = {}
        for d in (*PARTNERS, 0):
            (value,) = call(
                partial(pack_body, d), [((body + 3 * RUN, cols), F32)], "pack", 10, 2,
                (core_at, place_z, factors, *parts, sources, column, kernel),
                whole,
            )
            sent[d] = value
        got = exchange(sent)
        sent = sent[0]
        mixed = [((SIDE, body + RUN, cols), F32)]
        tables = (table_in, table_out)
        if outer == 0:
            sent, spread_kernel = call(
                partial(mix_body, True), mixed + [((SIDE * body, cols), F32)], "mix", 16, 0,
                (sent, *got, *tables), [pltpu.VMEM((SIDE, LANES, RUN), F32)],
            )
        else:
            (sent,) = call(
                partial(mix_body, False), mixed, "mix", 16, 0,
                (sent, *got, *tables, spread_kernel),
            )
        back = [sent, *exchange(sent)]
        last = outer == OUTER - 1
        if last:
            (amplitude,) = call(
                amplitude_body, [(right_side.shape, F32)], "amplitude", 10, 1,
                (core_at, factors, *parts, sources, column), whole,
            )
        sources, *rest = call(
            unpack_body,
            [(right_side.shape, F32)] + ([] if last else [((rows, wide), BF16)]),
            "unpack", 4, 1, (place_z, right_side, *back),
        )
        if not last:
            (rounded,) = rest
    return (amplitude, sources)


def solution(mesh):
    return jax.shard_map(
        shards,
        mesh=mesh,
        in_specs=(
            P("freq", "fac", None),
            P("fac", None),
            P("freq", "fac"),
            P("freq", "fac"),
            P(),
            P(),
        ),
        out_specs=(P("freq", "fac", None), P("freq", "fac", None)),
        check_vma=False,
    )
```

```python
from functools import partial

import jax
import jax.numpy as jnp
from jax import lax
from jax.experimental import pallas as pl
from jax.experimental.pallas import tpu as pltpu
from jax.sharding import PartitionSpec as P

OUTER = 2
INNER = 2
F32 = jnp.float32
BF16 = jnp.bfloat16
F16 = jnp.float16
SIDE = 4
RUN = 16
LANES = 128
PARTNERS = (2, 1, 3)
ARRIVALS = (0, 1, 3, 2)
INTERPRET = False


def place(y, x, k):
    return (y * SIDE + x) * 2 + k


def along(d, first):
    pairs = []
    for y in range(SIDE):
        for x in range(SIDE):
            for k in range(2):
                on_x = (k == 0) == first
                there = place(y, x ^ d, k) if on_x else place(y ^ d, x, k)
                pairs.append((place(y, x, k), there))
    return pairs


CORES = [(i, i ^ 1) for i in range(2 * SIDE * SIDE)]


def swap(d):
    return [(z, z ^ d) for z in range(SIDE)]


def scale_of(peak):
    power = jnp.ceil(jnp.log2(jnp.maximum(peak, 1e-30))) - 14.0
    return power, jnp.exp2(-power)


def round_body(right_ref, rounded_ref):
    nf, rows, cols = right_ref.shape
    for f in range(nf):
        rounded_ref[:, f * cols : (f + 1) * cols] = right_ref[f].astype(BF16)


def gather_parts(core_ref, mine_ref, other_ref, whole):
    half = mine_ref.shape[0]
    core = core_ref[0]
    whole[pl.ds(pl.multiple_of(core * half, half), half), :] = mine_ref[...]
    whole[pl.ds(pl.multiple_of((1 - core) * half, half), half), :] = other_ref[...]


def join_body(spot_ref, piece0, piece1, piece3, piece2, out_ref):
    chunk = piece0.shape[0]
    for d, piece in enumerate((piece0, piece1, piece2, piece3)):
        at = pl.ds(pl.multiple_of((spot_ref[0] ^ d) * chunk, chunk), chunk)
        out_ref[at, :] = piece[...]


def ladder_body(core_ref, factors_ref, mine_ref, other_ref, sources_ref, weight_ref,
                rounded_ref, whole):
    nf, rows, cols = sources_ref.shape
    gather_parts(core_ref, mine_ref, other_ref, whole)
    span = rows // SIDE

    def step(r, carry):
        at = pl.ds(pl.multiple_of(r * span, RUN), span)
        spread = jnp.dot(factors_ref[at, :], whole[...], preferred_element_type=F32)
        for f in range(nf):
            lanes = slice(f * cols, (f + 1) * cols)
            value = sources_ref[f, at, :] + weight_ref[at, f : f + 1] * spread[:, lanes]
            rounded_ref[at, lanes] = value.astype(BF16)
        return carry

    lax.fori_loop(0, SIDE, step, 0)


def pack_body(d, core_ref, z_ref, factors_ref, mine_ref, other_ref, sources_ref,
              weight_ref, kernel_ref, sent_ref, whole):
    nf, rows, cols = sources_ref.shape
    quarter = rows // SIDE
    body = nf * quarter
    there = z_ref[0] ^ d
    at = pl.ds(pl.multiple_of(there * quarter, RUN), quarter)
    gather_parts(core_ref, mine_ref, other_ref, whole)
    spread = jnp.dot(factors_ref[at, :], whole[...], preferred_element_type=F32)
    peak = jnp.zeros((RUN, cols), F32)
    for f in range(nf):
        lanes = slice(f * cols, (f + 1) * cols)
        value = sources_ref[f, at, :] + weight_ref[at, f : f + 1] * spread[:, lanes]
        for g in range(quarter // RUN):
            tile = value[g * RUN : (g + 1) * RUN]
            sent_ref[(g * nf + f) * RUN : (g * nf + f + 1) * RUN, :] = tile
            peak = jnp.maximum(peak, jnp.abs(tile))
    kernel = kernel_ref[there]
    high = kernel.astype(BF16).astype(F32)
    sent_ref[body + RUN : body + 2 * RUN, :] = high
    sent_ref[body + 2 * RUN :, :] = kernel - high
    if d:
        peak = jnp.max(jnp.max(peak, axis=0, keepdims=True), axis=1, keepdims=True)
        power, scale = scale_of(jnp.broadcast_to(peak, (1, cols)))
        sent_ref[:body, :] = sent_ref[:body, :] * jnp.broadcast_to(scale, (body, cols))
        sent_ref[body : body + RUN, :] = jnp.broadcast_to(power, (RUN, cols))


def amplitude_body(core_ref, factors_ref, mine_ref, other_ref, sources_ref, weight_ref,
                   amplitude_ref, whole):
    nf, rows, cols = sources_ref.shape
    gather_parts(core_ref, mine_ref, other_ref, whole)
    span = rows // SIDE

    def step(r, carry):
        at = pl.ds(pl.multiple_of(r * span, RUN), span)
        spread = jnp.dot(factors_ref[at, :], whole[...], preferred_element_type=F32)
        for f in range(nf):
            lanes = slice(f * cols, (f + 1) * cols)
            amplitude_ref[f, at, :] = sources_ref[f, at, :] + weight_ref[at, f : f + 1] * spread[:, lanes]
        return carry

    lax.fori_loop(0, SIDE, step, 0)


def expand_body(nf, strips, table_ref, kernel_ref, turned):
    body, cols = kernel_ref.shape
    table = table_ref[body + RUN : body + 2 * RUN, :] + table_ref[body + 2 * RUN :, :]
    turned[...] = table.T
    each = LANES // RUN
    groups = body // (nf * RUN)
    for strip in range(strips):

        def step(j, carry, strip=strip):
            rows = turned[pl.ds(pl.multiple_of(j * RUN, RUN), RUN), :]
            for f in range(nf):
                column = rows[:, f * strips + strip : f * strips + strip + 1]
                spot = ((strip * each + j) * nf + f) * RUN
                kernel_ref[pl.ds(pl.multiple_of(spot, RUN), RUN), :] = jnp.broadcast_to(column, (RUN, cols))
            return carry

        lax.fori_loop(0, min(each, groups - strip * each), step, 0)


def mix_body(own_ref, got1, got3, got2, into_ref, out_ref, kernel0, kernel1, kernel3, kernel2, sent_ref):
    body, cols = kernel0.shape
    size = into_ref.shape[1]
    part = size // SIDE
    got = (got1, got2, got3)
    kernel_refs = (kernel0, kernel1, kernel2, kernel3)
    groups = body // part
    wide = max(w for w in (2, 4, 6, 9) if groups % w == 0)
    gains = [jnp.exp2(jnp.broadcast_to(g[body : body + 1, :], (part, cols))) for g in got]

    def apply(table, value):
        high = value.astype(BF16)
        low = (value - high.astype(F32)).astype(BF16)
        both = jnp.dot(table[...], high, preferred_element_type=F32)
        rest = jnp.dot(table[:size, :], low, preferred_element_type=F32)
        return both[:size] + (both[size:] + rest)

    def step(g, peaks):
        sides = []
        kernels = []
        for half in range(wide):
            at = pl.ds(pl.multiple_of((wide * g + half) * part, part), part)
            sides.append(
                jnp.concatenate(
                    [own_ref[at, :]] + [r[at, :] * s for r, s in zip(got, gains)], axis=0
                )
            )
            kernels.append(jnp.concatenate([r[at, :] for r in kernel_refs], axis=0))
        timed = apply(into_ref, jnp.concatenate(sides, axis=1))
        renewed = apply(out_ref, jnp.concatenate(kernels, axis=1) * timed)
        fresh = list(peaks)
        for half in range(wide):
            at = pl.ds(pl.multiple_of((wide * g + half) * part, part), part)
            for d in range(SIDE):
                tile = renewed[d * part : (d + 1) * part, half * cols : (half + 1) * cols]
                sent_ref[d, at, :] = tile
                if d:
                    fresh[d - 1] = jnp.maximum(fresh[d - 1], jnp.abs(tile))
        return tuple(fresh)

    start = tuple(jnp.zeros((part, cols), F32) for _ in range(3))
    peaks = lax.fori_loop(0, groups // wide, step, start)
    for d, peak in enumerate(peaks, 1):
        peak = jnp.max(jnp.max(peak, axis=0, keepdims=True), axis=1, keepdims=True)
        power, scale = scale_of(jnp.broadcast_to(peak, (1, cols)))
        sent_ref[d, :body, :] = sent_ref[d, :body, :] * jnp.broadcast_to(scale, (body, cols))
        sent_ref[d, body:, :] = jnp.broadcast_to(power, (RUN, cols))


def unpack_body(z_ref, right_ref, own_ref, got1, got3, got2, sources_ref, *rounded):
    nf, rows, cols = right_ref.shape
    quarter = rows // SIDE
    z = z_ref[0]
    body = nf * quarter
    for d, ref in enumerate((own_ref, got1, got2, got3)):
        base = (z ^ d) * quarter
        gain = jnp.exp2(jnp.broadcast_to(ref[body : body + 1, :], (RUN, cols))) if d else None

        def step(g, carry, d=d, base=base, ref=ref, gain=gain):
            at = pl.ds(pl.multiple_of(base + g * RUN, RUN), RUN)
            for f in range(nf):
                spot = pl.ds(pl.multiple_of((g * nf + f) * RUN, RUN), RUN)
                tile = ref[spot, :] * gain if d else ref[0, spot, :]
                tile = right_ref[f, at, :] + tile
                sources_ref[f, at, :] = tile
                for rounded_ref in rounded:
                    rounded_ref[at, f * cols : (f + 1) * cols] = tile.astype(BF16)
            return carry

        lax.fori_loop(0, quarter // RUN, step, 0)


def call(body, outs, name, limit, scalars=0, args=(), scratch=()):
    spec = pl.BlockSpec(memory_space=pltpu.VMEM)
    flat = pl.BlockSpec(memory_space=pltpu.SMEM)
    specs = [flat] * scalars + [spec] * (len(args) - scalars)
    return pl.pallas_call(
        body,
        out_shape=[jax.ShapeDtypeStruct(s, t) for s, t in outs],
        in_specs=specs,
        out_specs=[spec] * len(outs),
        scratch_shapes=list(scratch),
        compiler_params=pltpu.CompilerParams(vmem_limit_bytes=limit << 20),
        interpret=INTERPRET,
        name=name,
    )(*args)


def shards(right_side, factors, pair_weight, second_order, forward, backward):
    nf, rows, cols = right_side.shape
    naux = factors.shape[1]
    half = naux // 2
    chunk = half // SIDE
    quarter = rows // SIDE
    wide = nf * cols
    me = lax.axis_index("fac")
    z = lax.axis_index("freq")
    core = me % 2
    chip = me // 2
    spot = jnp.where(core == 0, chip % SIDE, chip // SIDE)
    spot_at = jnp.full((1,), spot, jnp.int32)
    factors_keep = lax.dynamic_slice(factors, (0, core * half), (rows, half))
    factors_send = lax.dynamic_slice(factors, (0, (1 - core) * half), (rows, half))

    def project(table, rounded):
        return lax.dot_general(
            table, rounded, (((0,), (0,)), ((), ())), preferred_element_type=F32
        )

    def reduce_all(rounded):
        sent = project(factors_send, rounded)
        got = lax.ppermute(sent, "fac", CORES)
        mine = project(factors_keep, rounded) + got
        own = lax.dynamic_slice(mine, (spot * chunk, 0), (chunk, wide))
        for d in PARTNERS:
            piece = lax.dynamic_slice(
                mine, ((spot ^ d) * chunk, 0), (chunk, wide)
            ).astype(BF16)
            own = own + lax.ppermute(piece, "fac", along(d, True)).astype(F32)
        own = own.astype(BF16)
        total = own.astype(F32)
        for d in ARRIVALS[1:]:
            total = total + lax.ppermute(own, "fac", along(d, False)).astype(F32)
        total = total.astype(BF16)
        pieces = {0: total}
        for d in PARTNERS:
            pieces[d] = lax.ppermute(total, "fac", along(d, True))
        (gathered,) = call(
            join_body, [((half, wide), BF16)], "join", 4, 1,
            (spot_at, *[pieces[d] for d in ARRIVALS]),
        )
        other = lax.ppermute(gathered, "fac", CORES)
        return gathered, other

    def exchange(sent):
        got = {}
        for d in PARTNERS:
            got[d] = lax.ppermute(sent[d].astype(F16), "freq", swap(d)).astype(F32)
        return [got[d] for d in ARRIVALS[1:]]

    body = nf * quarter
    size = SIDE * nf * RUN
    place_z = jnp.full((1,), z, jnp.int32)
    strips = -(-quarter // LANES)
    kernel = second_order.reshape(nf, SIDE, quarter).transpose(1, 0, 2)
    kernel = jnp.pad(kernel, ((0, 0), (0, 0), (0, strips * LANES - quarter)))
    kernel = kernel.reshape(SIDE, nf * strips, LANES)
    kernel = jnp.pad(kernel, ((0, 0), (0, RUN - nf * strips), (0, 0)))

    row = jnp.arange(size)
    ring_at, f_at = row // (nf * RUN), row // RUN % nf
    names = jnp.arange(SIDE * nf)
    source = ((z ^ ring_at) * nf + f_at)[:, None] == names[None, :]
    same = (row % RUN)[:, None] == (row % RUN)[None, :]

    def spread_table(left, table, right):
        left, right = left.astype(F32), right.astype(F32)
        full = jnp.einsum("it,tw,jw->ij", left, table, right, precision=lax.Precision.HIGHEST)
        full = jnp.where(same, full, 0.0)
        high = lax.reduce_precision(full, 8, 7)
        return jnp.concatenate([high, full - high], axis=0).astype(BF16)

    table_in = spread_table(source, forward, source)
    table_out = spread_table(source, backward, source)

    core_at = jnp.full((1,), core, jnp.int32)
    column = pair_weight.T
    whole = [pltpu.VMEM((naux, wide), BF16)]
    sources = right_side
    (rounded,) = call(round_body, [((rows, wide), BF16)], "round", 4, 0, (right_side,))
    for outer in range(OUTER):
        for inner in range(INNER - 1):
            parts = reduce_all(rounded)
            (rounded,) = call(
                ladder_body, [((rows, wide), BF16)], "ladder", 10, 1,
                (core_at, factors, *parts, sources, column),
                whole,
            )
        parts = reduce_all(rounded)
        sent = {}
        for d in (*PARTNERS, 0):
            (value,) = call(
                partial(pack_body, d), [((body + 3 * RUN, cols), F32)], "pack", 10, 2,
                (core_at, place_z, factors, *parts, sources, column, kernel),
                whole,
            )
            sent[d] = value
        got = exchange(sent)
        sent = sent[0]
        if outer == 0:
            kernels = [
                call(partial(expand_body, nf, strips), [((body, cols), F32)], "expand", 4, 0,
                     (block,), [pltpu.VMEM((LANES, RUN), F32)])[0]
                for block in (sent, *got)
            ]
        (sent,) = call(
            mix_body, [((SIDE, body + RUN, cols), F32)], "mix", 24, 0,
            (sent, *got, table_in, table_out, *kernels),
        )
        back = [sent, *exchange(sent)]
        last = outer == OUTER - 1
        if last:
            (amplitude,) = call(
                amplitude_body, [(right_side.shape, F32)], "amplitude", 10, 1,
                (core_at, factors, *parts, sources, column), whole,
            )
        sources, *rest = call(
            unpack_body,
            [(right_side.shape, F32)] + ([] if last else [((rows, wide), BF16)]),
            "unpack", 4, 1, (place_z, right_side, *back),
        )
        if not last:
            (rounded,) = rest
    return (amplitude, sources)


def solution(mesh):
    return jax.shard_map(
        shards,
        mesh=mesh,
        in_specs=(
            P("freq", "fac", None),
            P("fac", None),
            P("freq", "fac"),
            P("freq", "fac"),
            P(),
            P(),
        ),
        out_specs=(P("freq", "fac", None), P("freq", "fac", None)),
        check_vma=False,
    )
```

```python
from functools import partial

import jax
import jax.numpy as jnp
from jax import lax
from jax.experimental import pallas as pl
from jax.experimental.pallas import tpu as pltpu
from jax.sharding import PartitionSpec as P

OUTER = 2
INNER = 2
F32 = jnp.float32
BF16 = jnp.bfloat16
F16 = jnp.float16
SIDE = 4
RUN = 16
LANES = 128
PARTNERS = (2, 1, 3)
ARRIVALS = (0, 1, 3, 2)
INTERPRET = False


def place(y, x, k):
    return (y * SIDE + x) * 2 + k


def along(d, first):
    pairs = []
    for y in range(SIDE):
        for x in range(SIDE):
            for k in range(2):
                on_x = (k == 0) == first
                there = place(y, x ^ d, k) if on_x else place(y ^ d, x, k)
                pairs.append((place(y, x, k), there))
    return pairs


CORES = [(i, i ^ 1) for i in range(2 * SIDE * SIDE)]


def swap(d):
    return [(z, z ^ d) for z in range(SIDE)]


def scale_of(peak):
    power = jnp.ceil(jnp.log2(jnp.maximum(peak, 1e-30))) - 14.0
    return power, jnp.exp2(-power)


def round_body(right_ref, rounded_ref):
    nf, rows, cols = right_ref.shape
    for f in range(nf):
        rounded_ref[:, f * cols : (f + 1) * cols] = right_ref[f].astype(BF16)


def gather_parts(core_ref, mine_ref, other_ref, whole):
    half = mine_ref.shape[0]
    core = core_ref[0]
    whole[pl.ds(pl.multiple_of(core * half, half), half), :] = mine_ref[...]
    whole[pl.ds(pl.multiple_of((1 - core) * half, half), half), :] = other_ref[...]


def join_body(spot_ref, piece0, piece1, piece3, piece2, out_ref):
    chunk = piece0.shape[0]
    for d, piece in enumerate((piece0, piece1, piece2, piece3)):
        at = pl.ds(pl.multiple_of((spot_ref[0] ^ d) * chunk, chunk), chunk)
        out_ref[at, :] = piece[...]


def ladder_body(core_ref, factors_ref, mine_ref, other_ref, sources_ref, weight_ref,
                rounded_ref, whole):
    nf, rows, cols = sources_ref.shape
    gather_parts(core_ref, mine_ref, other_ref, whole)
    span = rows // SIDE

    def step(r, carry):
        at = pl.ds(pl.multiple_of(r * span, RUN), span)
        spread = jnp.dot(factors_ref[at, :], whole[...], preferred_element_type=F32)
        for f in range(nf):
            lanes = slice(f * cols, (f + 1) * cols)
            value = sources_ref[f, at, :] + weight_ref[at, f : f + 1] * spread[:, lanes]
            rounded_ref[at, lanes] = value.astype(BF16)
        return carry

    lax.fori_loop(0, SIDE, step, 0)


def pack_body(d, core_ref, z_ref, factors_ref, mine_ref, other_ref, sources_ref,
              weight_ref, kernel_ref, sent_ref, whole):
    nf, rows, cols = sources_ref.shape
    quarter = rows // SIDE
    body = nf * quarter
    there = z_ref[0] ^ d
    at = pl.ds(pl.multiple_of(there * quarter, RUN), quarter)
    gather_parts(core_ref, mine_ref, other_ref, whole)
    spread = jnp.dot(factors_ref[at, :], whole[...], preferred_element_type=F32)
    peak = jnp.zeros((RUN, cols), F32)
    for f in range(nf):
        lanes = slice(f * cols, (f + 1) * cols)
        value = sources_ref[f, at, :] + weight_ref[at, f : f + 1] * spread[:, lanes]
        for g in range(quarter // RUN):
            tile = value[g * RUN : (g + 1) * RUN]
            sent_ref[(g * nf + f) * RUN : (g * nf + f + 1) * RUN, :] = tile
            peak = jnp.maximum(peak, jnp.abs(tile))
    kernel = kernel_ref[there]
    high = kernel.astype(BF16).astype(F32)
    sent_ref[body + RUN : body + 2 * RUN, :] = high
    sent_ref[body + 2 * RUN :, :] = kernel - high
    if d:
        peak = jnp.max(jnp.max(peak, axis=0, keepdims=True), axis=1, keepdims=True)
        power, scale = scale_of(jnp.broadcast_to(peak, (1, cols)))
        sent_ref[:body, :] = sent_ref[:body, :] * jnp.broadcast_to(scale, (body, cols))
        sent_ref[body : body + RUN, :] = jnp.broadcast_to(power, (RUN, cols))


def amplitude_body(core_ref, factors_ref, mine_ref, other_ref, sources_ref, weight_ref,
                   amplitude_ref, whole):
    nf, rows, cols = sources_ref.shape
    gather_parts(core_ref, mine_ref, other_ref, whole)
    span = rows // SIDE

    def step(r, carry):
        at = pl.ds(pl.multiple_of(r * span, RUN), span)
        spread = jnp.dot(factors_ref[at, :], whole[...], preferred_element_type=F32)
        for f in range(nf):
            lanes = slice(f * cols, (f + 1) * cols)
            amplitude_ref[f, at, :] = sources_ref[f, at, :] + weight_ref[at, f : f + 1] * spread[:, lanes]
        return carry

    lax.fori_loop(0, SIDE, step, 0)


def expand_body(nf, strips, table_ref, kernel_ref, turned):
    body, cols = kernel_ref.shape
    table = table_ref[body + RUN : body + 2 * RUN, :] + table_ref[body + 2 * RUN :, :]
    turned[...] = table.T
    each = LANES // RUN
    groups = body // (nf * RUN)
    for strip in range(strips):

        def step(j, carry, strip=strip):
            rows = turned[pl.ds(pl.multiple_of(j * RUN, RUN), RUN), :]
            for f in range(nf):
                column = rows[:, f * strips + strip : f * strips + strip + 1]
                spot = ((strip * each + j) * nf + f) * RUN
                kernel_ref[pl.ds(pl.multiple_of(spot, RUN), RUN), :] = jnp.broadcast_to(column, (RUN, cols))
            return carry

        lax.fori_loop(0, min(each, groups - strip * each), step, 0)


def mix_body(own_ref, got1, got3, got2, into_ref, out_ref, kernel0, kernel1, kernel3, kernel2, sent_ref):
    body, cols = kernel0.shape
    size = into_ref.shape[1]
    part = size // SIDE
    got = (got1, got2, got3)
    kernel_refs = (kernel0, kernel1, kernel2, kernel3)
    groups = body // part
    wide = max(w for w in (2, 4, 6, 9) if groups % w == 0)
    gains = [jnp.exp2(jnp.broadcast_to(g[body : body + 1, :], (part, cols))) for g in got]

    def apply(table, value):
        high = value.astype(BF16)
        low = (value - high.astype(F32)).astype(BF16)
        both = jnp.dot(table[...], high, preferred_element_type=F32)
        rest = jnp.dot(table[:size, :], low, preferred_element_type=F32)
        return both[:size] + (both[size:] + rest)

    def step(g, peaks):
        sides = []
        kernels = []
        for half in range(wide):
            at = pl.ds(pl.multiple_of((wide * g + half) * part, part), part)
            sides.append(
                jnp.concatenate(
                    [own_ref[at, :]] + [r[at, :] * s for r, s in zip(got, gains)], axis=0
                )
            )
            kernels.append(jnp.concatenate([r[at, :] for r in kernel_refs], axis=0))
        timed = apply(into_ref, jnp.concatenate(sides, axis=1))
        renewed = apply(out_ref, jnp.concatenate(kernels, axis=1) * timed)
        fresh = list(peaks)
        for half in range(wide):
            at = pl.ds(pl.multiple_of((wide * g + half) * part, part), part)
            for d in range(SIDE):
                tile = renewed[d * part : (d + 1) * part, half * cols : (half + 1) * cols]
                sent_ref[d, at, :] = tile
                if d:
                    fresh[d - 1] = jnp.maximum(fresh[d - 1], jnp.abs(tile))
        return tuple(fresh)

    start = tuple(jnp.zeros((part, cols), F32) for _ in range(3))
    peaks = lax.fori_loop(0, groups // wide, step, start)
    for d, peak in enumerate(peaks, 1):
        peak = jnp.max(jnp.max(peak, axis=0, keepdims=True), axis=1, keepdims=True)
        power, scale = scale_of(jnp.broadcast_to(peak, (1, cols)))
        sent_ref[d, :body, :] = sent_ref[d, :body, :] * jnp.broadcast_to(scale, (body, cols))
        sent_ref[d, body:, :] = jnp.broadcast_to(power, (RUN, cols))


def unpack_body(z_ref, right_ref, own_ref, got1, got3, got2, sources_ref, *rounded):
    nf, rows, cols = right_ref.shape
    quarter = rows // SIDE
    z = z_ref[0]
    body = nf * quarter
    for d, ref in enumerate((own_ref, got1, got2, got3)):
        base = (z ^ d) * quarter
        gain = jnp.exp2(jnp.broadcast_to(ref[body : body + 1, :], (RUN, cols))) if d else None

        def step(g, carry, d=d, base=base, ref=ref, gain=gain):
            at = pl.ds(pl.multiple_of(base + g * RUN, RUN), RUN)
            for f in range(nf):
                spot = pl.ds(pl.multiple_of((g * nf + f) * RUN, RUN), RUN)
                tile = ref[spot, :] * gain if d else ref[0, spot, :]
                tile = right_ref[f, at, :] + tile
                sources_ref[f, at, :] = tile
                for rounded_ref in rounded:
                    rounded_ref[at, f * cols : (f + 1) * cols] = tile.astype(BF16)
            return carry

        lax.fori_loop(0, quarter // RUN, step, 0)


def call(body, outs, name, limit, scalars=0, args=(), scratch=()):
    spec = pl.BlockSpec(memory_space=pltpu.VMEM)
    flat = pl.BlockSpec(memory_space=pltpu.SMEM)
    specs = [flat] * scalars + [spec] * (len(args) - scalars)
    return pl.pallas_call(
        body,
        out_shape=[jax.ShapeDtypeStruct(s, t) for s, t in outs],
        in_specs=specs,
        out_specs=[spec] * len(outs),
        scratch_shapes=list(scratch),
        compiler_params=pltpu.CompilerParams(vmem_limit_bytes=limit << 20),
        interpret=INTERPRET,
        name=name,
    )(*args)


def shards(right_side, factors, pair_weight, second_order, forward, backward):
    nf, rows, cols = right_side.shape
    naux = factors.shape[1]
    half = naux // 2
    chunk = half // SIDE
    quarter = rows // SIDE
    wide = nf * cols
    me = lax.axis_index("fac")
    z = lax.axis_index("freq")
    core = me % 2
    chip = me // 2
    spot = jnp.where(core == 0, chip % SIDE, chip // SIDE)
    spot_at = jnp.full((1,), spot, jnp.int32)
    factors_keep = lax.dynamic_slice(factors, (0, core * half), (rows, half))
    factors_send = lax.dynamic_slice(factors, (0, (1 - core) * half), (rows, half))

    def project(table, rounded):
        return lax.dot_general(
            table, rounded, (((0,), (0,)), ((), ())), preferred_element_type=F32
        )

    def reduce_all(rounded):
        sent = project(factors_send, rounded).astype(BF16)
        got = lax.ppermute(sent, "fac", CORES)
        mine = project(factors_keep, rounded) + got.astype(F32)
        own = lax.dynamic_slice(mine, (spot * chunk, 0), (chunk, wide))
        for d in PARTNERS:
            piece = lax.dynamic_slice(
                mine, ((spot ^ d) * chunk, 0), (chunk, wide)
            ).astype(BF16)
            own = own + lax.ppermute(piece, "fac", along(d, True)).astype(F32)
        own = own.astype(BF16)
        total = own.astype(F32)
        for d in ARRIVALS[1:]:
            total = total + lax.ppermute(own, "fac", along(d, False)).astype(F32)
        total = total.astype(BF16)
        pieces = {0: total}
        for d in PARTNERS:
            pieces[d] = lax.ppermute(total, "fac", along(d, True))
        (gathered,) = call(
            join_body, [((half, wide), BF16)], "join", 4, 1,
            (spot_at, *[pieces[d] for d in ARRIVALS]),
        )
        other = lax.ppermute(gathered, "fac", CORES)
        return gathered, other

    def exchange(sent):
        got = {}
        for d in PARTNERS:
            got[d] = lax.ppermute(sent[d].astype(F16), "freq", swap(d)).astype(F32)
        return [got[d] for d in ARRIVALS[1:]]

    body = nf * quarter
    size = SIDE * nf * RUN
    place_z = jnp.full((1,), z, jnp.int32)
    strips = -(-quarter // LANES)
    kernel = second_order.reshape(nf, SIDE, quarter).transpose(1, 0, 2)
    kernel = jnp.pad(kernel, ((0, 0), (0, 0), (0, strips * LANES - quarter)))
    kernel = kernel.reshape(SIDE, nf * strips, LANES)
    kernel = jnp.pad(kernel, ((0, 0), (0, RUN - nf * strips), (0, 0)))

    row = jnp.arange(size)
    ring_at, f_at = row // (nf * RUN), row // RUN % nf
    names = jnp.arange(SIDE * nf)
    source = ((z ^ ring_at) * nf + f_at)[:, None] == names[None, :]
    same = (row % RUN)[:, None] == (row % RUN)[None, :]

    def spread_table(left, table, right):
        left, right = left.astype(F32), right.astype(F32)
        full = jnp.einsum("it,tw,jw->ij", left, table, right, precision=lax.Precision.HIGHEST)
        full = jnp.where(same, full, 0.0)
        high = lax.reduce_precision(full, 8, 7)
        return jnp.concatenate([high, full - high], axis=0).astype(BF16)

    table_in = spread_table(source, forward, source)
    table_out = spread_table(source, backward, source)

    core_at = jnp.full((1,), core, jnp.int32)
    column = pair_weight.T
    whole = [pltpu.VMEM((naux, wide), BF16)]
    sources = right_side
    (rounded,) = call(round_body, [((rows, wide), BF16)], "round", 4, 0, (right_side,))
    for outer in range(OUTER):
        for inner in range(INNER - 1):
            parts = reduce_all(rounded)
            (rounded,) = call(
                ladder_body, [((rows, wide), BF16)], "ladder", 10, 1,
                (core_at, factors, *parts, sources, column),
                whole,
            )
        parts = reduce_all(rounded)
        sent = {}
        for d in (*PARTNERS, 0):
            (value,) = call(
                partial(pack_body, d), [((body + 3 * RUN, cols), F32)], "pack", 10, 2,
                (core_at, place_z, factors, *parts, sources, column, kernel),
                whole,
            )
            sent[d] = value
        got = exchange(sent)
        sent = sent[0]
        if outer == 0:
            kernels = [
                call(partial(expand_body, nf, strips), [((body, cols), F32)], "expand", 4, 0,
                     (block,), [pltpu.VMEM((LANES, RUN), F32)])[0]
                for block in (sent, *got)
            ]
        (sent,) = call(
            mix_body, [((SIDE, body + RUN, cols), F32)], "mix", 24, 0,
            (sent, *got, table_in, table_out, *kernels),
        )
        back = [sent, *exchange(sent)]
        last = outer == OUTER - 1
        if last:
            (amplitude,) = call(
                amplitude_body, [(right_side.shape, F32)], "amplitude", 10, 1,
                (core_at, factors, *parts, sources, column), whole,
            )
        sources, *rest = call(
            unpack_body,
            [(right_side.shape, F32)] + ([] if last else [((rows, wide), BF16)]),
            "unpack", 4, 1, (place_z, right_side, *back),
        )
        if not last:
            (rounded,) = rest
    return (amplitude, sources)


def solution(mesh):
    return jax.shard_map(
        shards,
        mesh=mesh,
        in_specs=(
            P("freq", "fac", None),
            P("fac", None),
            P("freq", "fac"),
            P("freq", "fac"),
            P(),
            P(),
        ),
        out_specs=(P("freq", "fac", None), P("freq", "fac", None)),
        check_vma=False,
    )
```

```python
from functools import partial

import jax
import jax.numpy as jnp
from jax import lax
from jax.experimental import pallas as pl
from jax.experimental.pallas import tpu as pltpu
from jax.sharding import PartitionSpec as P

OUTER = 2
INNER = 2
F32 = jnp.float32
BF16 = jnp.bfloat16
F16 = jnp.float16
SIDE = 4
RUN = 16
LANES = 128
PARTNERS = (2, 1, 3)
ARRIVALS = (0, 1, 3, 2)
INTERPRET = False


def place(y, x, k):
    return (y * SIDE + x) * 2 + k


def along(d, first):
    pairs = []
    for y in range(SIDE):
        for x in range(SIDE):
            for k in range(2):
                on_x = (k == 0) == first
                there = place(y, x ^ d, k) if on_x else place(y ^ d, x, k)
                pairs.append((place(y, x, k), there))
    return pairs


CORES = [(i, i ^ 1) for i in range(2 * SIDE * SIDE)]


def swap(d):
    return [(z, z ^ d) for z in range(SIDE)]


def scale_of(peak):
    power = jnp.ceil(jnp.log2(jnp.maximum(peak, 1e-30))) - 14.0
    return power, jnp.exp2(-power)


def round_body(core_ref, right_ref, factors_ref, rounded_ref, keep_ref, send_ref):
    nf, rows, cols = right_ref.shape
    half = keep_ref.shape[1]
    core = core_ref[0]
    keep_ref[...] = factors_ref[:, pl.ds(pl.multiple_of(core * half, half), half)]
    send_ref[...] = factors_ref[:, pl.ds(pl.multiple_of((1 - core) * half, half), half)]
    for f in range(nf):
        rounded_ref[:, f * cols : (f + 1) * cols] = right_ref[f].astype(BF16)


def gather_parts(core_ref, mine_ref, other_ref, whole):
    half = mine_ref.shape[0]
    core = core_ref[0]
    whole[pl.ds(pl.multiple_of(core * half, half), half), :] = mine_ref[...]
    whole[pl.ds(pl.multiple_of((1 - core) * half, half), half), :] = other_ref[...]


def join_body(spot_ref, piece0, piece1, piece3, piece2, out_ref):
    chunk = piece0.shape[0]
    for d, piece in enumerate((piece0, piece1, piece2, piece3)):
        at = pl.ds(pl.multiple_of((spot_ref[0] ^ d) * chunk, chunk), chunk)
        out_ref[at, :] = piece[...]


def ladder_body(core_ref, factors_ref, mine_ref, other_ref, sources_ref, weight_ref,
                rounded_ref, whole):
    nf, rows, cols = sources_ref.shape
    gather_parts(core_ref, mine_ref, other_ref, whole)
    span = rows // SIDE

    def step(r, carry):
        at = pl.ds(pl.multiple_of(r * span, RUN), span)
        spread = jnp.dot(factors_ref[at, :], whole[...], preferred_element_type=F32)
        for f in range(nf):
            lanes = slice(f * cols, (f + 1) * cols)
            value = sources_ref[f, at, :] + weight_ref[at, f : f + 1] * spread[:, lanes]
            rounded_ref[at, lanes] = value.astype(BF16)
        return carry

    lax.fori_loop(0, SIDE, step, 0)


def pack_body(d, core_ref, z_ref, factors_ref, mine_ref, other_ref, sources_ref,
              weight_ref, kernel_ref, sent_ref, whole):
    nf, rows, cols = sources_ref.shape
    quarter = rows // SIDE
    body = nf * quarter
    there = z_ref[0] ^ d
    at = pl.ds(pl.multiple_of(there * quarter, RUN), quarter)
    gather_parts(core_ref, mine_ref, other_ref, whole)
    spread = jnp.dot(factors_ref[at, :], whole[...], preferred_element_type=F32)
    peak = jnp.zeros((RUN, cols), F32)
    for f in range(nf):
        lanes = slice(f * cols, (f + 1) * cols)
        value = sources_ref[f, at, :] + weight_ref[at, f : f + 1] * spread[:, lanes]
        for g in range(quarter // RUN):
            tile = value[g * RUN : (g + 1) * RUN]
            sent_ref[(g * nf + f) * RUN : (g * nf + f + 1) * RUN, :] = tile
            peak = jnp.maximum(peak, jnp.abs(tile))
    kernel = kernel_ref[there]
    high = kernel.astype(BF16).astype(F32)
    sent_ref[body + RUN : body + 2 * RUN, :] = high
    sent_ref[body + 2 * RUN :, :] = kernel - high
    if d:
        peak = jnp.max(jnp.max(peak, axis=0, keepdims=True), axis=1, keepdims=True)
        power, scale = scale_of(jnp.broadcast_to(peak, (1, cols)))
        sent_ref[:body, :] = sent_ref[:body, :] * jnp.broadcast_to(scale, (body, cols))
        sent_ref[body : body + RUN, :] = jnp.broadcast_to(power, (RUN, cols))


def amplitude_body(core_ref, factors_ref, mine_ref, other_ref, sources_ref, weight_ref,
                   amplitude_ref, whole):
    nf, rows, cols = sources_ref.shape
    gather_parts(core_ref, mine_ref, other_ref, whole)
    span = rows // SIDE

    def step(r, carry):
        at = pl.ds(pl.multiple_of(r * span, RUN), span)
        spread = jnp.dot(factors_ref[at, :], whole[...], preferred_element_type=F32)
        for f in range(nf):
            lanes = slice(f * cols, (f + 1) * cols)
            amplitude_ref[f, at, :] = sources_ref[f, at, :] + weight_ref[at, f : f + 1] * spread[:, lanes]
        return carry

    lax.fori_loop(0, SIDE, step, 0)


def expand_body(nf, strips, table_ref, kernel_ref, turned):
    body, cols = kernel_ref.shape
    table = table_ref[body + RUN : body + 2 * RUN, :] + table_ref[body + 2 * RUN :, :]
    turned[...] = table.T
    each = LANES // RUN
    groups = body // (nf * RUN)
    for strip in range(strips):

        def step(j, carry, strip=strip):
            rows = turned[pl.ds(pl.multiple_of(j * RUN, RUN), RUN), :]
            for f in range(nf):
                column = rows[:, f * strips + strip : f * strips + strip + 1]
                spot = ((strip * each + j) * nf + f) * RUN
                kernel_ref[pl.ds(pl.multiple_of(spot, RUN), RUN), :] = jnp.broadcast_to(column, (RUN, cols))
            return carry

        lax.fori_loop(0, min(each, groups - strip * each), step, 0)


def mix_body(own_ref, got1, got3, got2, into_ref, out_ref, kernel0, kernel1, kernel3, kernel2, sent_ref):
    body, cols = kernel0.shape
    size = into_ref.shape[1]
    part = size // SIDE
    got = (got1, got2, got3)
    kernel_refs = (kernel0, kernel1, kernel2, kernel3)
    groups = body // part
    wide = max(w for w in (2, 4, 6, 9) if groups % w == 0)
    gains = [jnp.exp2(jnp.broadcast_to(g[body : body + 1, :], (part, cols))) for g in got]

    def apply(table, value):
        high = value.astype(BF16)
        low = (value - high.astype(F32)).astype(BF16)
        both = jnp.dot(table[...], high, preferred_element_type=F32)
        rest = jnp.dot(table[:size, :], low, preferred_element_type=F32)
        return both[:size] + (both[size:] + rest)

    def step(g, peaks):
        sides = []
        kernels = []
        for half in range(wide):
            at = pl.ds(pl.multiple_of((wide * g + half) * part, part), part)
            sides.append(
                jnp.concatenate(
                    [own_ref[at, :]] + [r[at, :] * s for r, s in zip(got, gains)], axis=0
                )
            )
            kernels.append(jnp.concatenate([r[at, :] for r in kernel_refs], axis=0))
        timed = apply(into_ref, jnp.concatenate(sides, axis=1))
        renewed = apply(out_ref, jnp.concatenate(kernels, axis=1) * timed)
        fresh = list(peaks)
        for half in range(wide):
            at = pl.ds(pl.multiple_of((wide * g + half) * part, part), part)
            for d in range(SIDE):
                tile = renewed[d * part : (d + 1) * part, half * cols : (half + 1) * cols]
                sent_ref[d, at, :] = tile
                if d:
                    fresh[d - 1] = jnp.maximum(fresh[d - 1], jnp.abs(tile))
        return tuple(fresh)

    start = tuple(jnp.zeros((part, cols), F32) for _ in range(3))
    peaks = lax.fori_loop(0, groups // wide, step, start)
    for d, peak in enumerate(peaks, 1):
        peak = jnp.max(jnp.max(peak, axis=0, keepdims=True), axis=1, keepdims=True)
        power, scale = scale_of(jnp.broadcast_to(peak, (1, cols)))
        sent_ref[d, :body, :] = sent_ref[d, :body, :] * jnp.broadcast_to(scale, (body, cols))
        sent_ref[d, body:, :] = jnp.broadcast_to(power, (RUN, cols))


def unpack_body(z_ref, right_ref, own_ref, got1, got3, got2, sources_ref, *rounded):
    nf, rows, cols = right_ref.shape
    quarter = rows // SIDE
    z = z_ref[0]
    body = nf * quarter
    for d, ref in enumerate((own_ref, got1, got2, got3)):
        base = (z ^ d) * quarter
        gain = jnp.exp2(jnp.broadcast_to(ref[body : body + 1, :], (RUN, cols))) if d else None

        def step(g, carry, d=d, base=base, ref=ref, gain=gain):
            at = pl.ds(pl.multiple_of(base + g * RUN, RUN), RUN)
            for f in range(nf):
                spot = pl.ds(pl.multiple_of((g * nf + f) * RUN, RUN), RUN)
                tile = ref[spot, :] * gain if d else ref[0, spot, :]
                tile = right_ref[f, at, :] + tile
                sources_ref[f, at, :] = tile
                for rounded_ref in rounded:
                    rounded_ref[at, f * cols : (f + 1) * cols] = tile.astype(BF16)
            return carry

        lax.fori_loop(0, quarter // RUN, step, 0)


def call(body, outs, name, limit, scalars=0, args=(), scratch=()):
    spec = pl.BlockSpec(memory_space=pltpu.VMEM)
    flat = pl.BlockSpec(memory_space=pltpu.SMEM)
    specs = [flat] * scalars + [spec] * (len(args) - scalars)
    return pl.pallas_call(
        body,
        out_shape=[jax.ShapeDtypeStruct(s, t) for s, t in outs],
        in_specs=specs,
        out_specs=[spec] * len(outs),
        scratch_shapes=list(scratch),
        compiler_params=pltpu.CompilerParams(vmem_limit_bytes=limit << 20),
        interpret=INTERPRET,
        name=name,
    )(*args)


def shards(right_side, factors, pair_weight, second_order, forward, backward):
    nf, rows, cols = right_side.shape
    naux = factors.shape[1]
    half = naux // 2
    chunk = half // SIDE
    quarter = rows // SIDE
    wide = nf * cols
    me = lax.axis_index("fac")
    z = lax.axis_index("freq")
    core = me % 2
    chip = me // 2
    spot = jnp.where(core == 0, chip % SIDE, chip // SIDE)
    spot_at = jnp.full((1,), spot, jnp.int32)
    core_at = jnp.full((1,), core, jnp.int32)
    rounded, first_keep, first_send = call(
        round_body, [((rows, wide), BF16)] + [((rows, half), BF16)] * 2, "round", 6, 1,
        (core_at, right_side, factors),
    )

    factors_keep = lax.dynamic_slice(factors, (0, core * half), (rows, half))
    factors_send = lax.dynamic_slice(factors, (0, (1 - core) * half), (rows, half))

    def project(table, rounded):
        return lax.dot_general(
            table, rounded, (((0,), (0,)), ((), ())), preferred_element_type=F32
        )

    def reduce_all(rounded, keep=factors_keep, send=factors_send):
        sent = project(send, rounded).astype(BF16)
        got = lax.ppermute(sent, "fac", CORES)
        mine = project(keep, rounded) + got.astype(F32)
        own = lax.dynamic_slice(mine, (spot * chunk, 0), (chunk, wide))
        for d in PARTNERS:
            piece = lax.dynamic_slice(
                mine, ((spot ^ d) * chunk, 0), (chunk, wide)
            ).astype(BF16)
            own = own + lax.ppermute(piece, "fac", along(d, True)).astype(F32)
        own = own.astype(BF16)
        total = own.astype(F32)
        for d in ARRIVALS[1:]:
            total = total + lax.ppermute(own, "fac", along(d, False)).astype(F32)
        total = total.astype(BF16)
        pieces = {0: total}
        for d in PARTNERS:
            pieces[d] = lax.ppermute(total, "fac", along(d, True))
        (gathered,) = call(
            join_body, [((half, wide), BF16)], "join", 4, 1,
            (spot_at, *[pieces[d] for d in ARRIVALS]),
        )
        other = lax.ppermute(gathered, "fac", CORES)
        return gathered, other

    def exchange(sent):
        got = {}
        for d in PARTNERS:
            got[d] = lax.ppermute(sent[d].astype(F16), "freq", swap(d)).astype(F32)
        return [got[d] for d in ARRIVALS[1:]]

    body = nf * quarter
    size = SIDE * nf * RUN
    place_z = jnp.full((1,), z, jnp.int32)
    strips = -(-quarter // LANES)
    kernel = second_order.reshape(nf, SIDE, quarter).transpose(1, 0, 2)
    kernel = jnp.pad(kernel, ((0, 0), (0, 0), (0, strips * LANES - quarter)))
    kernel = kernel.reshape(SIDE, nf * strips, LANES)
    kernel = jnp.pad(kernel, ((0, 0), (0, RUN - nf * strips), (0, 0)))

    row = jnp.arange(size)
    ring_at, f_at = row // (nf * RUN), row // RUN % nf
    names = jnp.arange(SIDE * nf)
    source = ((z ^ ring_at) * nf + f_at)[:, None] == names[None, :]
    same = (row % RUN)[:, None] == (row % RUN)[None, :]

    def spread_table(left, table, right):
        left, right = left.astype(F32), right.astype(F32)
        full = jnp.einsum("it,tw,jw->ij", left, table, right, precision=lax.Precision.HIGHEST)
        full = jnp.where(same, full, 0.0)
        high = lax.reduce_precision(full, 8, 7)
        return jnp.concatenate([high, full - high], axis=0).astype(BF16)

    table_in = spread_table(source, forward, source)
    table_out = spread_table(source, backward, source)

    column = pair_weight.T
    whole = [pltpu.VMEM((naux, wide), BF16)]
    sources = right_side
    for outer in range(OUTER):
        for inner in range(INNER - 1):
            if outer + inner == 0:
                parts = reduce_all(rounded, first_keep, first_send)
            else:
                parts = reduce_all(rounded)
            (rounded,) = call(
                ladder_body, [((rows, wide), BF16)], "ladder", 10, 1,
                (core_at, factors, *parts, sources, column),
                whole,
            )
        parts = reduce_all(rounded)
        sent = {}
        for d in (*PARTNERS, 0):
            (value,) = call(
                partial(pack_body, d), [((body + 3 * RUN, cols), F32)], "pack", 10, 2,
                (core_at, place_z, factors, *parts, sources, column, kernel),
                whole,
            )
            sent[d] = value
        got = exchange(sent)
        sent = sent[0]
        if outer == 0:
            kernels = [
                call(partial(expand_body, nf, strips), [((body, cols), F32)], "expand", 4, 0,
                     (block,), [pltpu.VMEM((LANES, RUN), F32)])[0]
                for block in (sent, *got)
            ]
        (sent,) = call(
            mix_body, [((SIDE, body + RUN, cols), F32)], "mix", 24, 0,
            (sent, *got, table_in, table_out, *kernels),
        )
        back = [sent, *exchange(sent)]
        last = outer == OUTER - 1
        if last:
            (amplitude,) = call(
                amplitude_body, [(right_side.shape, F32)], "amplitude", 10, 1,
                (core_at, factors, *parts, sources, column), whole,
            )
        sources, *rest = call(
            unpack_body,
            [(right_side.shape, F32)] + ([] if last else [((rows, wide), BF16)]),
            "unpack", 4, 1, (place_z, right_side, *back),
        )
        if not last:
            (rounded,) = rest
    return (amplitude, sources)


def solution(mesh):
    return jax.shard_map(
        shards,
        mesh=mesh,
        in_specs=(
            P("freq", "fac", None),
            P("fac", None),
            P("freq", "fac"),
            P("freq", "fac"),
            P(),
            P(),
        ),
        out_specs=(P("freq", "fac", None), P("freq", "fac", None)),
        check_vma=False,
    )
```

```python
from functools import partial

import jax
import jax.numpy as jnp
from jax import lax
from jax.experimental import pallas as pl
from jax.experimental.pallas import tpu as pltpu
from jax.sharding import PartitionSpec as P

OUTER = 2
INNER = 2
F32 = jnp.float32
BF16 = jnp.bfloat16
F16 = jnp.float16
SIDE = 4
RUN = 16
LANES = 128
PARTNERS = (2, 1, 3)
ARRIVALS = (0, 1, 3, 2)
INTERPRET = False


def place(y, x, k):
    return (y * SIDE + x) * 2 + k


def along(d, first):
    pairs = []
    for y in range(SIDE):
        for x in range(SIDE):
            for k in range(2):
                on_x = (k == 0) == first
                there = place(y, x ^ d, k) if on_x else place(y ^ d, x, k)
                pairs.append((place(y, x, k), there))
    return pairs


CORES = [(i, i ^ 1) for i in range(2 * SIDE * SIDE)]


def swap(d):
    return [(z, z ^ d) for z in range(SIDE)]


def scale_of(peak):
    power = jnp.ceil(jnp.log2(jnp.maximum(peak, 1e-30))) - 14.0
    return power, jnp.exp2(-power)


def round_body(right_ref, rounded_ref):
    nf, rows, cols = right_ref.shape
    for f in range(nf):
        rounded_ref[:, f * cols : (f + 1) * cols] = right_ref[f].astype(BF16)


def gather_parts(core_ref, mine_ref, other_ref, whole):
    half = mine_ref.shape[0]
    core = core_ref[0]
    whole[pl.ds(pl.multiple_of(core * half, half), half), :] = mine_ref[...]
    whole[pl.ds(pl.multiple_of((1 - core) * half, half), half), :] = other_ref[...]


def join_body(spot_ref, piece0, piece1, piece3, piece2, out_ref):
    chunk = piece0.shape[0]
    for d, piece in enumerate((piece0, piece1, piece2, piece3)):
        at = pl.ds(pl.multiple_of((spot_ref[0] ^ d) * chunk, chunk), chunk)
        out_ref[at, :] = piece[...]


def ladder_body(core_ref, factors_ref, mine_ref, other_ref, sources_ref, weight_ref,
                rounded_ref, whole):
    nf, rows, cols = sources_ref.shape
    gather_parts(core_ref, mine_ref, other_ref, whole)
    span = rows // SIDE

    def step(r, carry):
        at = pl.ds(pl.multiple_of(r * span, RUN), span)
        spread = jnp.dot(factors_ref[at, :], whole[...], preferred_element_type=F32)
        for f in range(nf):
            lanes = slice(f * cols, (f + 1) * cols)
            value = sources_ref[f, at, :] + weight_ref[at, f : f + 1] * spread[:, lanes]
            rounded_ref[at, lanes] = value.astype(BF16)
        return carry

    lax.fori_loop(0, SIDE, step, 0)


def pack_body(d, core_ref, z_ref, factors_ref, mine_ref, other_ref, sources_ref,
              weight_ref, kernel_ref, sent_ref, whole):
    nf, rows, cols = sources_ref.shape
    quarter = rows // SIDE
    body = nf * quarter
    there = z_ref[0] ^ d
    at = pl.ds(pl.multiple_of(there * quarter, RUN), quarter)
    gather_parts(core_ref, mine_ref, other_ref, whole)
    spread = jnp.dot(factors_ref[at, :], whole[...], preferred_element_type=F32)
    peak = jnp.zeros((RUN, cols), F32)
    for f in range(nf):
        lanes = slice(f * cols, (f + 1) * cols)
        value = sources_ref[f, at, :] + weight_ref[at, f : f + 1] * spread[:, lanes]
        for g in range(quarter // RUN):
            tile = value[g * RUN : (g + 1) * RUN]
            sent_ref[(g * nf + f) * RUN : (g * nf + f + 1) * RUN, :] = tile
            peak = jnp.maximum(peak, jnp.abs(tile))
    if sent_ref.shape[0] > body + RUN:
        kernel = kernel_ref[there]
        high = kernel.astype(BF16).astype(F32)
        sent_ref[body + RUN : body + 2 * RUN, :] = high
        sent_ref[body + 2 * RUN :, :] = kernel - high
    if d:
        peak = jnp.max(jnp.max(peak, axis=0, keepdims=True), axis=1, keepdims=True)
        power, scale = scale_of(jnp.broadcast_to(peak, (1, cols)))
        sent_ref[:body, :] = sent_ref[:body, :] * jnp.broadcast_to(scale, (body, cols))
        sent_ref[body : body + RUN, :] = jnp.broadcast_to(power, (RUN, cols))


def amplitude_body(core_ref, factors_ref, mine_ref, other_ref, sources_ref, weight_ref,
                   amplitude_ref, whole):
    nf, rows, cols = sources_ref.shape
    gather_parts(core_ref, mine_ref, other_ref, whole)
    span = rows // SIDE

    def step(r, carry):
        at = pl.ds(pl.multiple_of(r * span, RUN), span)
        spread = jnp.dot(factors_ref[at, :], whole[...], preferred_element_type=F32)
        for f in range(nf):
            lanes = slice(f * cols, (f + 1) * cols)
            amplitude_ref[f, at, :] = sources_ref[f, at, :] + weight_ref[at, f : f + 1] * spread[:, lanes]
        return carry

    lax.fori_loop(0, SIDE, step, 0)


def expand_body(nf, strips, table_ref, kernel_ref, turned):
    body, cols = kernel_ref.shape
    table = table_ref[body + RUN : body + 2 * RUN, :] + table_ref[body + 2 * RUN :, :]
    turned[...] = table.T
    each = LANES // RUN
    groups = body // (nf * RUN)
    for strip in range(strips):

        def step(j, carry, strip=strip):
            rows = turned[pl.ds(pl.multiple_of(j * RUN, RUN), RUN), :]
            for f in range(nf):
                column = rows[:, f * strips + strip : f * strips + strip + 1]
                spot = ((strip * each + j) * nf + f) * RUN
                kernel_ref[pl.ds(pl.multiple_of(spot, RUN), RUN), :] = jnp.broadcast_to(column, (RUN, cols))
            return carry

        lax.fori_loop(0, min(each, groups - strip * each), step, 0)


def mix_body(own_ref, got1, got3, got2, into_ref, out_ref, kernel0, kernel1, kernel3, kernel2, sent_ref):
    body, cols = kernel0.shape
    size = into_ref.shape[1]
    part = size // SIDE
    got = (got1, got2, got3)
    kernel_refs = (kernel0, kernel1, kernel2, kernel3)
    groups = body // part
    wide = max(w for w in (2, 4, 6, 9) if groups % w == 0)
    gains = [jnp.exp2(jnp.broadcast_to(g[body : body + 1, :], (part, cols))) for g in got]

    def apply(table, value):
        high = value.astype(BF16)
        low = (value - high.astype(F32)).astype(BF16)
        both = jnp.dot(table[...], high, preferred_element_type=F32)
        rest = jnp.dot(table[:size, :], low, preferred_element_type=F32)
        return both[:size] + (both[size:] + rest)

    def step(g, peaks):
        sides = []
        kernels = []
        for half in range(wide):
            at = pl.ds(pl.multiple_of((wide * g + half) * part, part), part)
            sides.append(
                jnp.concatenate(
                    [own_ref[at, :]] + [r[at, :] * s for r, s in zip(got, gains)], axis=0
                )
            )
            kernels.append(jnp.concatenate([r[at, :] for r in kernel_refs], axis=0))
        timed = apply(into_ref, jnp.concatenate(sides, axis=1))
        renewed = apply(out_ref, jnp.concatenate(kernels, axis=1) * timed)
        fresh = list(peaks)
        for half in range(wide):
            at = pl.ds(pl.multiple_of((wide * g + half) * part, part), part)
            for d in range(SIDE):
                tile = renewed[d * part : (d + 1) * part, half * cols : (half + 1) * cols]
                sent_ref[d, at, :] = tile
                if d:
                    fresh[d - 1] = jnp.maximum(fresh[d - 1], jnp.abs(tile))
        return tuple(fresh)

    start = tuple(jnp.zeros((part, cols), F32) for _ in range(3))
    peaks = lax.fori_loop(0, groups // wide, step, start)
    for d, peak in enumerate(peaks, 1):
        peak = jnp.max(jnp.max(peak, axis=0, keepdims=True), axis=1, keepdims=True)
        power, scale = scale_of(jnp.broadcast_to(peak, (1, cols)))
        sent_ref[d, :body, :] = sent_ref[d, :body, :] * jnp.broadcast_to(scale, (body, cols))
        sent_ref[d, body:, :] = jnp.broadcast_to(power, (RUN, cols))


def unpack_body(z_ref, right_ref, own_ref, got1, got3, got2, sources_ref, *rounded):
    nf, rows, cols = right_ref.shape
    quarter = rows // SIDE
    z = z_ref[0]
    body = nf * quarter
    for d, ref in enumerate((own_ref, got1, got2, got3)):
        base = (z ^ d) * quarter
        gain = jnp.exp2(jnp.broadcast_to(ref[body : body + 1, :], (RUN, cols))) if d else None

        def step(g, carry, d=d, base=base, ref=ref, gain=gain):
            at = pl.ds(pl.multiple_of(base + g * RUN, RUN), RUN)
            for f in range(nf):
                spot = pl.ds(pl.multiple_of((g * nf + f) * RUN, RUN), RUN)
                tile = ref[spot, :] * gain if d else ref[0, spot, :]
                tile = right_ref[f, at, :] + tile
                sources_ref[f, at, :] = tile
                for rounded_ref in rounded:
                    rounded_ref[at, f * cols : (f + 1) * cols] = tile.astype(BF16)
            return carry

        lax.fori_loop(0, quarter // RUN, step, 0)


def call(body, outs, name, limit, scalars=0, args=(), scratch=()):
    spec = pl.BlockSpec(memory_space=pltpu.VMEM)
    flat = pl.BlockSpec(memory_space=pltpu.SMEM)
    specs = [flat] * scalars + [spec] * (len(args) - scalars)
    return pl.pallas_call(
        body,
        out_shape=[jax.ShapeDtypeStruct(s, t) for s, t in outs],
        in_specs=specs,
        out_specs=[spec] * len(outs),
        scratch_shapes=list(scratch),
        compiler_params=pltpu.CompilerParams(vmem_limit_bytes=limit << 20),
        interpret=INTERPRET,
        name=name,
    )(*args)


def shards(right_side, factors, pair_weight, second_order, forward, backward):
    nf, rows, cols = right_side.shape
    naux = factors.shape[1]
    half = naux // 2
    chunk = half // SIDE
    quarter = rows // SIDE
    wide = nf * cols
    me = lax.axis_index("fac")
    z = lax.axis_index("freq")
    core = me % 2
    chip = me // 2
    spot = jnp.where(core == 0, chip % SIDE, chip // SIDE)
    spot_at = jnp.full((1,), spot, jnp.int32)
    factors_keep = lax.dynamic_slice(factors, (0, core * half), (rows, half))
    factors_send = lax.dynamic_slice(factors, (0, (1 - core) * half), (rows, half))

    def project(table, rounded):
        return lax.dot_general(
            table, rounded, (((0,), (0,)), ((), ())), preferred_element_type=F32
        )

    def reduce_all(rounded):
        sent = project(factors_send, rounded).astype(BF16)
        got = lax.ppermute(sent, "fac", CORES)
        mine = project(factors_keep, rounded) + got.astype(F32)
        own = lax.dynamic_slice(mine, (spot * chunk, 0), (chunk, wide))
        for d in PARTNERS:
            piece = lax.dynamic_slice(
                mine, ((spot ^ d) * chunk, 0), (chunk, wide)
            ).astype(BF16)
            own = own + lax.ppermute(piece, "fac", along(d, True)).astype(F32)
        own = own.astype(BF16)
        total = own.astype(F32)
        for d in ARRIVALS[1:]:
            total = total + lax.ppermute(own, "fac", along(d, False)).astype(F32)
        total = total.astype(BF16)
        pieces = {0: total}
        for d in PARTNERS:
            pieces[d] = lax.ppermute(total, "fac", along(d, True))
        (gathered,) = call(
            join_body, [((half, wide), BF16)], "join", 4, 1,
            (spot_at, *[pieces[d] for d in ARRIVALS]),
        )
        other = lax.ppermute(gathered, "fac", CORES)
        return gathered, other

    def exchange(sent):
        got = {}
        for d in PARTNERS:
            got[d] = lax.ppermute(sent[d].astype(F16), "freq", swap(d)).astype(F32)
        return [got[d] for d in ARRIVALS[1:]]

    body = nf * quarter
    size = SIDE * nf * RUN
    place_z = jnp.full((1,), z, jnp.int32)
    strips = -(-quarter // LANES)
    kernel = second_order.reshape(nf, SIDE, quarter).transpose(1, 0, 2)
    kernel = jnp.pad(kernel, ((0, 0), (0, 0), (0, strips * LANES - quarter)))
    kernel = kernel.reshape(SIDE, nf * strips, LANES)
    kernel = jnp.pad(kernel, ((0, 0), (0, RUN - nf * strips), (0, 0)))

    row = jnp.arange(size)
    ring_at, f_at = row // (nf * RUN), row // RUN % nf
    names = jnp.arange(SIDE * nf)
    source = ((z ^ ring_at) * nf + f_at)[:, None] == names[None, :]
    same = (row % RUN)[:, None] == (row % RUN)[None, :]

    def spread_table(left, table, right):
        left, right = left.astype(F32), right.astype(F32)
        full = jnp.einsum("it,tw,jw->ij", left, table, right, precision=lax.Precision.HIGHEST)
        full = jnp.where(same, full, 0.0)
        high = lax.reduce_precision(full, 8, 7)
        return jnp.concatenate([high, full - high], axis=0).astype(BF16)

    table_in = spread_table(source, forward, source)
    table_out = spread_table(source, backward, source)

    core_at = jnp.full((1,), core, jnp.int32)
    column = pair_weight.T
    whole = [pltpu.VMEM((naux, wide), BF16)]
    sources = right_side
    (rounded,) = call(round_body, [((rows, wide), BF16)], "round", 4, 0, (right_side,))
    for outer in range(OUTER):
        for inner in range(INNER - 1):
            parts = reduce_all(rounded)
            (rounded,) = call(
                ladder_body, [((rows, wide), BF16)], "ladder", 10, 1,
                (core_at, factors, *parts, sources, column),
                whole,
            )
        parts = reduce_all(rounded)
        sent = {}
        for d in (*PARTNERS, 0):
            (value,) = call(
                partial(pack_body, d), [((body + (1 if outer else 3) * RUN, cols), F32)], "pack", 10, 2,
                (core_at, place_z, factors, *parts, sources, column, kernel),
                whole,
            )
            sent[d] = value
        got = exchange(sent)
        sent = sent[0]
        if outer == 0:
            kernels = [
                call(partial(expand_body, nf, strips), [((body, cols), F32)], "expand", 4, 0,
                     (block,), [pltpu.VMEM((LANES, RUN), F32)])[0]
                for block in (sent, *got)
            ]
        (sent,) = call(
            mix_body, [((SIDE, body + RUN, cols), F32)], "mix", 24, 0,
            (sent, *got, table_in, table_out, *kernels),
        )
        back = [sent, *exchange(sent)]
        last = outer == OUTER - 1
        if last:
            (amplitude,) = call(
                amplitude_body, [(right_side.shape, F32)], "amplitude", 10, 1,
                (core_at, factors, *parts, sources, column), whole,
            )
        sources, *rest = call(
            unpack_body,
            [(right_side.shape, F32)] + ([] if last else [((rows, wide), BF16)]),
            "unpack", 4, 1, (place_z, right_side, *back),
        )
        if not last:
            (rounded,) = rest
    return (amplitude, sources)


def solution(mesh):
    return jax.shard_map(
        shards,
        mesh=mesh,
        in_specs=(
            P("freq", "fac", None),
            P("fac", None),
            P("freq", "fac"),
            P("freq", "fac"),
            P(),
            P(),
        ),
        out_specs=(P("freq", "fac", None), P("freq", "fac", None)),
        check_vma=False,
    )
```
